32 devices in a mesh: groups: 2 (over x), seq: 16 (over z, y, core).
Axes of the slice: x: 2, y: 2, z: 4, core: 2. Of those that a mesh axis runs over, the one named last changes fastest.
Arguments:
- queries: bfloat16 [6, 16, 16, 2560], P('groups', 'seq'), parts along dimension 0, may hold values from -6 to 6
- keys: bfloat16 [6, 16, 16, 2560], P('groups', 'seq'), parts along dimension 0, may hold values from -6 to 6
- values: bfloat16 [6, 16, 16, 2560], P('groups', 'seq'), parts along dimension 0, may hold values from -6 to 6
- stream: bfloat16 [6, 16, 16, 2560], P('groups', 'seq'), parts along dimension 0, may hold values from -3 to 3
- head_weight: bfloat16 [2560, 64], replicated, may hold values from -0.125 to 0.125
- conv_in_weight: bfloat16 [3, 3, 3, 16, 384], replicated, may hold values from -0.3125 to 0.3125
- norm_gain: float32 [384], replicated, may hold values from 0.5 to 1.5
- norm_shift: float32 [384], replicated, may hold values from -3 to 3
- conv_mid_weight: bfloat16 [3, 3, 3, 384, 384], replicated, may hold values from -0.0625 to 0.0625
Outputs:
- decoded: bfloat16 [6, 32, 32, 384], P('groups', 'seq'), parts along dimension 0
The draws below stay inside these ranges and needn't reach their ends.
There are 2 independent parts, one for each index of `groups`. The reference program is written for one: setup_inputs(seed, part) draws one part's arguments, and reference() takes and returns one part's arrays. A program takes and returns all parts, laid end to end along the dimension named above; an argument that names none is the same for every part. Nothing has to cross between parts.
All inputs are finite; a program needn't handle non-finite values.
Results may differ from the reference program's by a relative error of at most 0.01.
Values may be sent and summed in bfloat16 or wider, within the bound.
A program may use at most 128 MiB of HBM per device.

```python
import jax
import jax.numpy as jnp
from jax import lax

HEADS = 20
HD = 128
LAT = 16
CH = 384
GROUPS = 32
FR = 3
COLS = 16
TROWS = 16


def drawn_field(key, factor):
    drawn = jax.random.normal(key, (FR, TROWS, COLS, HEADS, HD), jnp.float32)
    return jnp.clip(drawn * factor, -6.0, 6.0)


def draw_queries(key, part):
    field = drawn_field(jax.random.fold_in(key, 1), 2.0)
    return field.reshape(FR, TROWS, COLS, HEADS * HD).astype(jnp.bfloat16)


def draw_keys(key, part):
    field = drawn_field(jax.random.fold_in(key, 2), 1.0)
    return field.reshape(FR, TROWS, COLS, HEADS * HD).astype(jnp.bfloat16)


def draw_stream(key, part):
    width = HEADS * HD
    noise_key = jax.random.fold_in(key, 7)
    common_key = jax.random.fold_in(key, 8)
    place = jnp.arange(TROWS, dtype=jnp.float32) / max(TROWS - 1, 1)
    noise = jnp.clip(jax.random.normal(noise_key, (FR, TROWS, COLS, width), jnp.float32), -6.0, 6.0)
    rising = 0.5 + 2.5 * place
    common = jnp.clip(jax.random.normal(common_key, (width,), jnp.float32), -3.0, 3.0)
    field = rising[None, :, None, None] * (0.05 * noise + 0.15 * common)
    return field.astype(jnp.bfloat16)


def steps_of(rng, dims, cuts, low, high):
    factor_of, own = 1.0, jax.random.fold_in(rng, 6)
    for axis_at, shards_of in cuts:
        steps = jnp.exp(jax.random.uniform(jax.random.fold_in(own, axis_at), (shards_of,), jnp.float32, low / len(cuts), high / len(cuts)))
        factor_of = factor_of * jnp.repeat(steps, dims[axis_at] // shards_of).reshape([-1 if axis == axis_at else 1 for axis in range(len(dims))])
    return factor_of


def centred(own_key, dims, deviation, limit, shards=(), kind=jnp.bfloat16):
    values = jax.random.normal(own_key, dims, jnp.float32) * deviation
    if len(shards) > 0:
        values = steps_of(own_key, dims, shards, -0.22, 0.18) * values
    return jnp.clip(values, min=-limit, max=limit).astype(kind)


def setup_inputs(seed: int = 0, part: int = 0) -> dict:
    streams_of = jax.random.split(jax.random.key(seed), 10)
    own_keys = jax.random.split(jax.random.fold_in(streams_of[9], part), 10)
    return {
        "queries": draw_queries(jax.random.fold_in(jax.random.fold_in(streams_of[9], part), 71), part),
        "keys": draw_keys(jax.random.fold_in(jax.random.fold_in(streams_of[9], part), 71), part),
        "values": centred(own_keys[2], (FR, TROWS, COLS, HEADS * HD), 1.0, 6.0, ((1, 16),)),
        "stream": draw_stream(jax.random.fold_in(jax.random.fold_in(streams_of[9], part), 71), part),
        "head_weight": centred(streams_of[4], (HEADS * HD, 4 * LAT), (HEADS * HD) ** -0.5, 0.125),
        "conv_in_weight": centred(streams_of[5], (3, 3, 3, LAT, CH), (27 * LAT) ** -0.5, 0.3125),
        "norm_gain": jnp.clip(1.0 + 0.1 * jax.random.normal(streams_of[6], (CH,), jnp.float32), 0.5, 1.5),
        "norm_shift": centred(streams_of[7], (CH,), 0.5, 3.0, (), jnp.float32),
        "conv_mid_weight": centred(streams_of[8], (3, 3, 3, CH, CH), (27 * CH) ** -0.5, 0.0625),
    }


def conv_taps(padded, weight, frames, rows, cols):
    inner = padded.shape[-1]
    total = jnp.zeros((frames * rows * cols, weight.shape[-1]), jnp.float32)
    for step_t in range(3):
        for step_h in range(3):
            for step_w in range(3):
                piece = padded[step_t:step_t + frames, step_h:step_h + rows, step_w:step_w + cols, :].reshape(-1, inner)
                total = total + jnp.dot(piece, weight[step_t, step_h, step_w], preferred_element_type=jnp.float32)
    return total.reshape(frames, rows, cols, -1)

def pad_causal(field):
    return jnp.pad(field, ((2, 0), (1, 1), (1, 1), (0, 0)))

def reference(queries, keys, values, stream, head_weight, conv_in_weight, norm_gain, norm_shift, conv_mid_weight):
    frames, trows, cols, width = queries.shape
    depth = width // HEADS
    query_flat = queries.reshape(-1, HEADS, depth)
    key_flat = keys.reshape(-1, HEADS, depth)
    value_flat = values.reshape(-1, HEADS, depth)
    scale = 1.0 / depth ** 0.5

    def one_head(head):
        query_head = lax.dynamic_index_in_dim(query_flat, head, 1, keepdims=False)
        key_head = lax.dynamic_index_in_dim(key_flat, head, 1, keepdims=False)
        value_head = lax.dynamic_index_in_dim(value_flat, head, 1, keepdims=False)
        scores = jnp.dot(query_head, key_head.T, preferred_element_type=jnp.float32) * scale
        top = lax.optimization_barrier(jnp.max(scores, axis=-1, keepdims=True))
        expo = jnp.exp(scores - top)
        total = lax.optimization_barrier(jnp.sum(expo, axis=-1, keepdims=True))
        summed = jnp.dot(expo.astype(jnp.bfloat16), value_head, preferred_element_type=jnp.float32)
        return (summed / total).astype(jnp.bfloat16)
    heads_out = lax.map(one_head, jnp.arange(HEADS, dtype=jnp.int32))
    attended = jnp.transpose(heads_out, (1, 0, 2)).reshape(-1, width)
    latent = jnp.dot(stream.reshape(-1, width), head_weight, preferred_element_type=jnp.float32) + jnp.dot(attended, head_weight, preferred_element_type=jnp.float32)
    latent = latent.reshape(frames, trows, cols, 2, 2, -1).transpose(0, 1, 3, 2, 4, 5)
    latent = latent.reshape(frames, 2 * trows, 2 * cols, -1).astype(jnp.bfloat16)
    rows, wide = (2 * trows, 2 * cols)
    first = conv_taps(pad_causal(latent), conv_in_weight, frames, rows, wide)
    grouped = first.reshape(frames, rows, wide, GROUPS, -1)
    mean = lax.optimization_barrier(jnp.mean(grouped, axis=(0, 1, 2, 4)))
    centered = grouped - mean[:, None]
    variance = lax.optimization_barrier(jnp.mean(centered * centered, axis=(0, 1, 2, 4)))
    normed = (centered / jnp.sqrt(variance + 1e-06)[:, None]).reshape(frames, rows, wide, -1)
    active = jax.nn.silu(normed * norm_gain + norm_shift).astype(jnp.bfloat16)
    second = conv_taps(pad_causal(active), conv_mid_weight, frames, rows, wide)
    return (first + second).astype(jnp.bfloat16)
```

```python
import functools

import jax
import jax.numpy as jnp
from jax import lax
from jax.experimental import pallas as pl
from jax.experimental.pallas import tpu as pltpu
from jax.sharding import PartitionSpec as P

HEADS = 20
GROUPS = 32
QUARTERS = 4
LAT = 16
NT = (((1,), (1,)), ((), ()))


def dot(a, b):
    return jnp.dot(a, b, preferred_element_type=jnp.float32)


def dot_t(a, b):
    return lax.dot_general(a, b, NT, preferred_element_type=jnp.float32)


def body(
    n,
    frames,
    cols,
    q_ref,
    k_ref,
    v_ref,
    stream_hbm,
    head_hbm,
    wi_hbm,
    gain_ref,
    shift_ref,
    wm_hbm,
    out_ref,
    stream_ref,
    head_ref,
    wi_ref,
    qbuf,
    kv,
    sums,
    part,
    lbuf,
    tbuf,
    w4,
    wm,
    gmat,
    first,
    act,
    acc,
    woven,
    sbuf,
    zsend,
    zq,
    zkv,
    loc,
    ysend,
    yrecv,
    csend,
    crecv,
    lsend,
    lrecv,
    tsend,
    trecv,
    ssend,
    srecv,
    wsem,
    isem,
):
    A = QUARTERS
    B = n // A
    BH = B // 2
    H = HEADS // A
    tok = frames * cols
    hd = q_ref.shape[1] // HEADS
    ch = gain_ref.shape[0]
    half = tok // 2
    scale = 1.0 / hd**0.5
    me = lax.axis_index("seq")
    a = me // B
    b = me % B
    bh = b // 2
    core = b % 2
    sibling = me + 1 - 2 * core

    def remote(src, dst, ssem, rsem, to):
        return pltpu.make_async_remote_copy(
            src_ref=src,
            dst_ref=dst,
            send_sem=ssem,
            recv_sem=rsem,
            device_id={"seq": to},
            device_id_type=pl.DeviceIdType.MESH,
        )

    def drain(ref, sem):
        pltpu.make_async_copy(ref, ref, sem).wait()

    def columns(quarter, h):
        return pl.ds(pl.multiple_of((quarter * H + h) * hd, hd), hd)

    loads = [
        pltpu.make_async_copy(src, dst, isem.at[i])
        for i, (src, dst) in enumerate(
            ((wi_hbm, wi_ref), (stream_hbm, stream_ref), (head_hbm, head_ref))
        )
    ]
    for load in loads:
        load.start()
    tbuf[...] = jnp.zeros_like(tbuf)
    barrier = pltpu.get_barrier_semaphore()

    partners = [lax.rem(a + d, A) * B + b for d in range(1, A)]
    partners += [a * B + lax.rem(bh + d, BH) * 2 + core for d in range(1, BH)]
    partners.append(sibling)
    for to in partners:
        pl.semaphore_signal(
            barrier, inc=1, device_id={"seq": to}, device_id_type=pl.DeviceIdType.MESH
        )
    pl.semaphore_wait(barrier, len(partners))

    @pl.loop(0, H)
    def _(h):
        for d in range(1, A):
            to = lax.rem(a + d, A)
            cut = columns(to, h)
            peer = to * B + b
            remote(k_ref.at[:, cut], kv.at[h, b, 0, a], zsend.at[0], zkv.at[h], peer).start()
            remote(v_ref.at[:, cut], kv.at[h, b, 1, a], zsend.at[0], zkv.at[h], peer).start()

    @pl.loop(0, H)
    def _(h):
        for d in range(1, A):
            to = lax.rem(a + d, A)
            cut = columns(to, h)
            peer = to * B + b
            remote(q_ref.at[:, cut], qbuf.at[h, a], zsend.at[1], zq.at[h], peer).start()

    @pl.loop(0, H)
    def _(h):
        cut = columns(a, h)
        pltpu.make_async_copy(k_ref.at[:, cut], kv.at[h, b, 0, a], zkv.at[h]).start()
        pltpu.make_async_copy(v_ref.at[:, cut], kv.at[h, b, 1, a], zkv.at[h]).start()
        pltpu.make_async_copy(q_ref.at[:, cut], qbuf.at[h, a], zq.at[h]).start()

    weights = pltpu.make_async_copy(wm_hbm, wm, wsem)
    weights.start()

    w4[...] = jnp.zeros_like(w4)
    loads[0].wait()
    for ta in range(3):
        for ri in range(2):
            for pc in range(2):
                for tb in range(3):
                    at = (ri + tb) * 4 * LAT + LAT * pc
                    to = (2 * ri + pc) * ch
                    w4[ta, at : at + 3 * LAT, to : to + ch] = wi_ref[3 * ta + tb]
    span = ch // GROUPS

    def group_of(axis):
        at = lax.broadcasted_iota(jnp.int32, (ch, ch), axis).astype(jnp.float32)
        return jnp.floor((at + 0.5) * (1.0 / span))

    gmat[...] = jnp.where(group_of(0) == group_of(1), 1.0, 0.0).astype(jnp.bfloat16)
    sums[...] = jnp.zeros_like(sums)
    loads[1].wait()
    loads[2].wait()
    streamed = dot_t(stream_ref[...], head_ref[...])

    def spread_on(h):
        for d in range(1, BH):
            theirs = lax.rem(bh + BH - d, BH) * 2 + core
            slab = kv.at[h, theirs]
            drain(slab, yrecv.at[h, d])
            remote(slab, slab, csend, crecv.at[h, d], sibling).start()

    @pl.loop(0, H)
    def _(h):
        slab = kv.at[h, b]
        drain(slab, zkv.at[h])
        for d in range(1, BH):
            to = a * B + lax.rem(bh + d, BH) * 2 + core
            remote(slab, slab, ysend, yrecv.at[h, d], to).start()
        remote(slab, slab, csend, crecv.at[h, 0], sibling).start()

        @pl.when(h >= 1)
        def _():
            spread_on(h - 1)

    @pl.loop(0, H)
    def _(h):
        @pl.when(h == 2)
        def _():
            spread_on(H - 1)

        for d in range(BH):
            theirs = lax.rem(bh + BH - d, BH) * 2 + 1 - core
            drain(kv.at[h, theirs], crecv.at[h, d])
        drain(qbuf.at[h], zq.at[h])
        query = qbuf[h].reshape(A * tok, hd)
        key = kv[h, :, 0].reshape(n * tok, hd)
        value = kv[h, :, 1].reshape(n * tok, hd)
        scores = dot_t(query, key) * scale
        top = jnp.max(scores, axis=-1, keepdims=True)
        expo = jnp.exp(scores - top)
        total = jnp.sum(expo, axis=-1, keepdims=True)
        out = (dot(expo.astype(jnp.bfloat16), value) / total).astype(jnp.bfloat16)
        sums[...] += dot_t(out, head_ref[:, columns(a, h)]).reshape(A, tok, 4 * LAT)

    part[...] = jnp.concatenate([sums[:, :half], sums[:, half:]], axis=2)
    for d in range(1, A):
        to = lax.rem(a + d, A)
        remote(part.at[to], lbuf.at[a], lsend, lrecv, to * B + b).start()
    lbuf[a] = part[a]
    drain(lbuf.at[0 : A - 1], lrecv)
    latent = jnp.concatenate([streamed[:half], streamed[half:]], axis=1)
    for d in range(A):
        latent = latent + lbuf[d]
    tbuf[1] = latent

    @pl.when(me > 0)
    def _():
        remote(tbuf.at[1], tbuf.at[2], tsend.at[0], trecv.at[1], me - 1).start()

    @pl.when(me < n - 1)
    def _():
        remote(tbuf.at[1], tbuf.at[0], tsend.at[1], trecv.at[0], me + 1).start()

    @pl.when(me > 0)
    def _():
        drain(tbuf.at[0], trecv.at[0])

    @pl.when(me < n - 1)
    def _():
        drain(tbuf.at[2], trecv.at[1])

    wide = 8 * LAT
    src = lax.broadcasted_iota(jnp.int32, (4 * LAT, wide), 0)
    dst = lax.broadcasted_iota(jnp.int32, (4 * LAT, wide), 1)
    wanted = dst // (4 * LAT) * 2 * LAT + (dst // LAT + 1) % 2 * LAT + dst % LAT
    chosen = jnp.where(src == wanted, 1.0, 0.0).astype(jnp.bfloat16)
    lines = []
    for row in range(3):
        packed = tbuf[row]
        lines += [packed[:, : 4 * LAT], packed[:, 4 * LAT :]]
    laid = dot(jnp.concatenate(lines, axis=0).astype(jnp.bfloat16), chosen)
    spot = lax.broadcasted_iota(jnp.int32, (3 * tok, wide), 0) % cols
    piece = lax.broadcasted_iota(jnp.int32, (3 * tok, wide), 1) // LAT % 4
    before = jnp.where(spot == 0, 0.0, pltpu.roll(laid, 1, 0))
    after = jnp.where(spot == cols - 1, 0.0, pltpu.roll(laid, 3 * tok - 1, 0))
    laid = jnp.where(piece == 0, before, jnp.where(piece == 3, after, laid)).astype(jnp.bfloat16)
    near = []
    for f in range(frames):
        for pair in range(2):
            at = pair * tok + f * cols
            near.append(
                jnp.concatenate([laid[at : at + cols], laid[at + tok : at + tok + cols]], axis=1)
            )
    near = jnp.concatenate(near, axis=0)
    first[...] = dot(near, w4[2])
    for ta in (1, 0):
        first[(2 - ta) * 2 * cols :] += dot(near[: (ta + 1) * 2 * cols], w4[ta])

    def conv(row, phase):
        at = (row % 2 * 2 + phase) * ch
        return jnp.concatenate(
            [
                first[(2 * f + row // 2) * cols : (2 * f + row // 2 + 1) * cols, at : at + ch]
                for f in range(frames)
            ],
            axis=0,
        )

    cells = 4 * tok

    def folded(parts):
        whole = parts[0] + parts[1] + parts[2] + parts[3]
        return jnp.sum(whole, axis=0, keepdims=True)

    own = [conv(1 + ri, pc) for ri in range(2) for pc in range(2)]
    mean = folded(own) / cells
    square = folded([(x - mean) * (x - mean) for x in own])
    pieces = ch // 128
    rows = [x[:, 128 * i : 128 * (i + 1)] for x in (mean, square) for i in range(pieces)]
    rows.append(jnp.zeros((8 - 2 * pieces, 128), jnp.float32))
    sbuf[me] = jnp.concatenate(rows, axis=0)

    @pl.loop(1, n)
    def _(d):
        remote(sbuf.at[me], sbuf.at[me], ssend, srecv, lax.rem(me + d, n)).start()

    drain(sbuf.at[0 : n - 1], srecv)

    def grouped(x):
        high = x.astype(jnp.bfloat16).astype(jnp.float32)
        rest = x - high
        middle = rest.astype(jnp.bfloat16).astype(jnp.float32)
        pieces = [high, middle, rest - middle, jnp.zeros((13, ch), jnp.float32)]
        split = jnp.concatenate(pieces, axis=0).astype(jnp.bfloat16)
        return jnp.sum(dot(split, gmat[...]), axis=0, keepdims=True)

    means = jnp.concatenate([sbuf[:, i] for i in range(pieces)], axis=1)
    squares = jnp.concatenate([sbuf[:, pieces + i] for i in range(pieces)], axis=1)
    middle = grouped(jnp.sum(means, axis=0, keepdims=True)) / (n * span)
    apart = means - middle
    spread = jnp.sum(squares + cells * (apart * apart), axis=0, keepdims=True)
    variance = grouped(spread) / (n * span * cells)
    root = jnp.sqrt(variance + 1e-06)

    spot = lax.broadcasted_iota(jnp.int32, (tok, ch), 0) % cols

    def place(row, x0, x1):
        left = jnp.where(spot == 0, 0.0, pltpu.roll(x1, 1, 0))
        right = jnp.where(spot == cols - 1, 0.0, pltpu.roll(x0, tok - 1, 0))
        act[:, row, :, 0:ch] = left.astype(jnp.bfloat16).reshape(frames, cols, ch)
        act[:, row, :, 3 * ch :] = right.astype(jnp.bfloat16).reshape(frames, cols, ch)

    gain = gain_ref[...].reshape(1, ch)
    shift = shift_ref[...].reshape(1, ch)

    gain = gain / root

    def active(row, phase):
        y = (conv(row, phase) - middle) * gain + shift
        y = y * jax.nn.sigmoid(y)
        if row == 0:
            y = jnp.where(me > 0, y, 0.0)
        if row == 3:
            y = jnp.where(me < n - 1, y, 0.0)
        return y

    for row in range(4):
        x0 = active(row, 0)
        x1 = active(row, 1)
        act[:, row, :, ch : 2 * ch] = x0.astype(jnp.bfloat16).reshape(frames, cols, ch)
        act[:, row, :, 2 * ch : 3 * ch] = x1.astype(jnp.bfloat16).reshape(frames, cols, ch)
        place(row, x0, x1)

    weights.wait()

    def tap(ta, tb):
        rows = []
        for f in range(ta + 1):
            for pc in range(2):
                rows.append(
                    act[f, tb : tb + 2, :, pc * ch : (pc + 3) * ch].reshape(2 * cols, 3 * ch)
                )
        return dot(jnp.concatenate(rows, axis=0), wm[3 * ta + tb])

    for tb in range(3):
        for ta in (2, 1, 0):
            if tb == 0 and ta == 2:
                acc[...] = tap(ta, tb)
            else:
                acc[(2 - ta) * 4 * cols :] += tap(ta, tb)

    for f in range(frames):
        for pc in range(2):
            for ri in range(2):
                at = ((f * 2 + pc) * 2 + ri) * cols
                base = own[2 * ri + pc][f * cols : (f + 1) * cols]
                total = base + acc[at : at + cols]
                lines = pl.ds((f * 2 + ri) * 2 * cols + pc, cols, stride=2)
                for i in range(pieces):
                    woven[i, lines] = total[:, 128 * i : 128 * (i + 1)]
    for i in range(pieces):
        out_ref[:, :, :, 128 * i : 128 * (i + 1)] = (
            woven[i].reshape(frames, 2, 2 * cols, 128).astype(jnp.bfloat16)
        )

    drain(kv.at[:, 0, :, 0 : A - 1], zsend.at[0])
    drain(qbuf.at[:, 0 : A - 1], zsend.at[1])
    if BH > 1:
        drain(kv.at[:, 0 : BH - 1], ysend)
    drain(kv.at[:, 0:BH], csend)
    drain(part.at[0 : A - 1], lsend)
    drain(sbuf.at[0 : n - 1], ssend)

    @pl.when(me > 0)
    def _():
        drain(tbuf.at[1], tsend.at[0])

    @pl.when(me < n - 1)
    def _():
        drain(tbuf.at[1], tsend.at[1])


def shards(
    n,
    queries,
    keys,
    values,
    stream,
    head_weight,
    conv_in_weight,
    norm_gain,
    norm_shift,
    conv_mid_weight,
):
    frames, rows_here, cols, width = queries.shape
    assert frames == 3 and rows_here == 1
    tok = frames * cols
    hd = width // HEADS
    ch = norm_gain.shape[0]
    A = QUARTERS
    B = n // A
    BH = B // 2
    H = HEADS // A
    bf16, f32 = jnp.bfloat16, jnp.float32
    vmem = pl.BlockSpec(memory_space=pltpu.VMEM)
    hbm = pl.BlockSpec(memory_space=pl.ANY)
    dma = pltpu.SemaphoreType.DMA
    operands = [
        pltpu.with_memory_space_constraint(x, pltpu.HBM)
        for x in (
            queries.reshape(tok, width),
            keys.reshape(tok, width),
            values.reshape(tok, width),
            stream.reshape(tok, width),
            head_weight.T,
            conv_in_weight.reshape(9, 3 * LAT, ch),
            norm_gain,
            norm_shift,
            conv_mid_weight.reshape(9, 3 * ch, ch),
        )
    ]
    out = pl.pallas_call(
        functools.partial(body, n, frames, cols),
        out_shape=jax.ShapeDtypeStruct((frames, 2, 2 * cols, ch), bf16),
        in_specs=[hbm, hbm, hbm, hbm, hbm, hbm, vmem, vmem, hbm],
        out_specs=vmem,
        scratch_shapes=[
            pltpu.VMEM((tok, width), bf16),
            pltpu.VMEM((4 * LAT, width), bf16),
            pltpu.VMEM((9, 3 * LAT, ch), bf16),
            pltpu.VMEM((H, A, tok, hd), bf16),
            pltpu.VMEM((H, B, 2, A, tok, hd), bf16),
            pltpu.VMEM((A, tok, 4 * LAT), f32),
            pltpu.VMEM((A, tok // 2, 8 * LAT), f32),
            pltpu.VMEM((A, tok // 2, 8 * LAT), f32),
            pltpu.VMEM((3, tok // 2, 8 * LAT), f32),
            pltpu.VMEM((3, 16 * LAT, 4 * ch), bf16),
            pltpu.VMEM((9, 3 * ch, ch), bf16),
            pltpu.VMEM((ch, ch), bf16),
            pltpu.VMEM((2 * tok, 4 * ch), f32),
            pltpu.VMEM((frames, 4, cols, 4 * ch), bf16),
            pltpu.VMEM((4 * tok, ch), f32),
            pltpu.VMEM((ch // 128, 4 * tok, 128), f32),
            pltpu.VMEM((n, 8, 128), f32),
            dma((2,)),
            dma((H,)),
            dma((H,)),
            dma,
            dma,
            dma((H, BH)),
            dma,
            dma((H, BH)),
            dma,
            dma,
            dma((2,)),
            dma((2,)),
            dma,
            dma,
            dma,
            dma((3,)),
        ],
        compiler_params=pltpu.CompilerParams(
            collective_id=0, has_side_effects=True, vmem_limit_bytes=44 * 2**20
        ),
        name="decode",
    )(*operands)
    return out


def solution(mesh):
    row = P("groups", "seq", None, None)
    return jax.shard_map(
        functools.partial(shards, mesh.shape["seq"]),
        mesh=mesh,
        in_specs=(row, row, row, row, P(), P(), P(), P(), P()),
        out_specs=row,
        check_vma=False,
    )
```

```python
import functools
import math

import jax
import jax.numpy as jnp
from jax import lax
from jax.experimental import pallas as pl
from jax.experimental.pallas import tpu as pltpu
from jax.sharding import PartitionSpec as P

HEADS = 20
GROUPS = 32
QUARTERS = 4
LAG = 3
WINDOW = 6
LAT = 16
NT = (((1,), (1,)), ((), ()))


def dot(a, b):
    return jnp.dot(a, b, preferred_element_type=jnp.float32)


def dot_t(a, b):
    return lax.dot_general(a, b, NT, preferred_element_type=jnp.float32)


def body(
    n,
    frames,
    cols,
    q_ref,
    k_ref,
    v_hbm,
    stream_hbm,
    head_hbm,
    wi_hbm,
    gain_hbm,
    shift_hbm,
    wm_hbm,
    out_ref,
    v_ref,
    gain_ref,
    shift_ref,
    stream_ref,
    head_ref,
    wi_ref,
    vsend,
    qbuf,
    kv,
    sums,
    part,
    lbuf,
    tbuf,
    w4,
    wm,
    gmat,
    first,
    act,
    acc,
    woven,
    sbuf,
    zsend,
    zq,
    zkv,
    loc,
    ysend,
    yrecv,
    csend,
    crecv,
    lsend,
    lrecv,
    tsend,
    trecv,
    ssend,
    srecv,
    wsem,
    isem,
):
    A = QUARTERS
    B = n // A
    BH = B // 2
    H = HEADS // A
    PAIRS = (H + 1) // 2
    ITEMS = H + PAIRS
    tok = frames * cols
    hd = q_ref.shape[1] // HEADS
    ch = gain_ref.shape[0]
    half = tok // 2
    scale = math.log2(math.e) / hd**0.5
    me = lax.axis_index("seq")
    a = me // B
    b = me % B
    bh = b // 2
    core = b % 2
    sibling = me + 1 - 2 * core

    def remote(src, dst, ssem, rsem, to):
        return pltpu.make_async_remote_copy(
            src_ref=src,
            dst_ref=dst,
            send_sem=ssem,
            recv_sem=rsem,
            device_id={"seq": to},
            device_id_type=pl.DeviceIdType.MESH,
        )

    def drain(ref, sem):
        pltpu.make_async_copy(ref, ref, sem).wait()

    def columns(quarter, h):
        return pl.ds(pl.multiple_of((quarter * H + h) * hd, hd), hd)

    def key_at(h):
        return h + (h + 1) // 2

    def value_at(p):
        return 3 * p + 1

    barrier = pltpu.get_barrier_semaphore()
    partners = [lax.rem(a + d, A) * B + b for d in range(1, A)]
    partners += [a * B + lax.rem(bh + d, BH) * 2 + core for d in range(1, BH)]
    partners.append(sibling)
    for to in partners:
        pl.semaphore_signal(
            barrier, inc=1, device_id={"seq": to}, device_id_type=pl.DeviceIdType.MESH
        )

    loads = [
        pltpu.make_async_copy(src, dst, isem.at[i])
        for i, (src, dst) in enumerate(
            (
                (v_hbm, v_ref),
                (head_hbm, head_ref),
                (wi_hbm, wi_ref),
                (stream_hbm, stream_ref),
                (gain_hbm, gain_ref),
                (shift_hbm, shift_ref),
            )
        )
    ]
    for load in loads:
        load.start()
    for h in range(H):
        cut = columns(a, h)
        pltpu.make_async_copy(k_ref.at[:, cut], kv.at[key_at(h), b, a], zkv.at[key_at(h)]).start()
        pltpu.make_async_copy(q_ref.at[:, cut], qbuf.at[h, a], zq.at[h]).start()

    loads[0].wait()
    loads[1].wait()
    upper = lax.broadcasted_iota(jnp.int32, (4 * LAT, 2 * hd), 1) < hd
    for quarter in range(A):
        for p in range(PAIRS):
            wide = min(2, H - 2 * p) * hd
            at = (quarter * H + 2 * p) * hd
            w = head_ref[:, at : at + wide]
            if wide > hd:
                zero = jnp.zeros_like(w)
                w = jnp.concatenate(
                    [jnp.where(upper, w, zero), jnp.where(upper, zero, w)], axis=0
                )
            else:
                w = jnp.concatenate([w, jnp.zeros_like(w)], axis=0)
            vsend[quarter, p] = dot_t(v_ref[:, at : at + wide], w).astype(jnp.bfloat16)
    for p in range(PAIRS):
        kv[value_at(p), b, a] = vsend[a, p]

    pl.semaphore_wait(barrier, len(partners))

    def scatter(j):
        for d in range(1, A):
            to = lax.rem(a + d, A)
            peer = to * B + b
            if j >= ITEMS:
                h = j - ITEMS
                src = q_ref.at[:, columns(to, h)]
                remote(src, qbuf.at[h, a], zsend.at[1], zq.at[h], peer).start()
            else:
                if j % 3 == 1:
                    src = vsend.at[to, j // 3]
                else:
                    src = k_ref.at[:, columns(to, j - (j + 1) // 3)]
                remote(src, kv.at[j, b, a], zsend.at[0], zkv.at[j], peer).start()

    for j in range(WINDOW):
        scatter(j)

    tbuf[...] = jnp.zeros_like(tbuf)
    weights = pltpu.make_async_copy(wm_hbm, wm, wsem)
    weights.start()

    w4[...] = jnp.zeros_like(w4)
    loads[2].wait()
    for ta in range(3):
        for ri in range(2):
            for pc in range(2):
                for tb in range(3):
                    at = (ri + tb) * 4 * LAT + LAT * pc
                    to = (2 * ri + pc) * ch
                    w4[ta, at : at + 3 * LAT, to : to + ch] = wi_ref[3 * ta + tb]
    span = ch // GROUPS

    def group_of(axis):
        at = lax.broadcasted_iota(jnp.int32, (ch, ch), axis).astype(jnp.float32)
        return jnp.floor((at + 0.5) * (1.0 / span))

    gmat[...] = jnp.where(group_of(0) == group_of(1), 1.0, 0.0).astype(jnp.bfloat16)
    sums[...] = jnp.zeros_like(sums)
    loads[3].wait()
    streamed = dot_t(stream_ref[...], head_ref[...])

    def spread_on(j):
        for d in range(1, BH):
            theirs = lax.rem(bh + BH - d, BH) * 2 + core
            slab = kv.at[j, theirs]
            drain(slab, yrecv.at[j, d])
            remote(slab, slab, csend, crecv.at[j, d], sibling).start()

    for j in range(ITEMS):
        slab = kv.at[j, b]
        drain(slab if j % 3 != 1 else kv.at[j, b, 0 : A - 1], zkv.at[j])
        if j + WINDOW < ITEMS + H:
            scatter(j + WINDOW)
        for d in range(1, BH):
            to = a * B + lax.rem(bh + d, BH) * 2 + core
            remote(slab, slab, ysend, yrecv.at[j, d], to).start()
        remote(slab, slab, csend, crecv.at[j, 0], sibling).start()
        if j >= LAG:
            spread_on(j - LAG)
    for j in range(ITEMS + WINDOW, ITEMS + H):
        scatter(j)
    for j in range(max(ITEMS - LAG, 0), ITEMS):
        spread_on(j)

    def gathered(j):
        for d in range(BH):
            theirs = lax.rem(bh + BH - d, BH) * 2 + 1 - core
            drain(kv.at[j, theirs], crecv.at[j, d])

    side = lax.broadcasted_iota(jnp.int32, (A * tok, 8 * LAT), 1) // (4 * LAT)

    for h in range(H):
        gathered(key_at(h))
        if h % 2 == 0:
            gathered(value_at(h // 2))
        drain(qbuf.at[h], zq.at[h])
        query = qbuf[h].reshape(A * tok, hd)
        key = kv[key_at(h)].reshape(n * tok, hd)
        value = kv[value_at(h // 2)].reshape(n * tok, 8 * LAT)
        scores = dot_t(query, key)
        top = jnp.max(scores, axis=-1, keepdims=True)
        expo = jnp.exp2((scores - top) * scale)
        total = jnp.sum(expo, axis=-1, keepdims=True)
        out = dot(expo.astype(jnp.bfloat16), value) / total
        sums[...] += jnp.where(side == h % 2, out, 0.0)

    whole = sums[...]
    whole = (whole + pltpu.roll(whole, 4 * LAT, 1)).reshape(A, tok, 8 * LAT)
    left = lax.broadcasted_iota(jnp.int32, (A, half, 8 * LAT), 2) < 4 * LAT
    part[...] = jnp.where(left, whole[:, :half], whole[:, half:])
    for d in range(1, A):
        to = lax.rem(a + d, A)
        remote(part.at[to], lbuf.at[a], lsend, lrecv, to * B + b).start()
    lbuf[a] = part[a]
    drain(lbuf.at[0 : A - 1], lrecv)
    latent = jnp.concatenate([streamed[:half], streamed[half:]], axis=1)
    for d in range(A):
        latent = latent + lbuf[d]
    tbuf[1] = latent

    @pl.when(me > 0)
    def _():
        remote(tbuf.at[1], tbuf.at[2], tsend.at[0], trecv.at[1], me - 1).start()

    @pl.when(me < n - 1)
    def _():
        remote(tbuf.at[1], tbuf.at[0], tsend.at[1], trecv.at[0], me + 1).start()

    @pl.when(me > 0)
    def _():
        drain(tbuf.at[0], trecv.at[0])

    @pl.when(me < n - 1)
    def _():
        drain(tbuf.at[2], trecv.at[1])

    wide = 8 * LAT
    src = lax.broadcasted_iota(jnp.int32, (4 * LAT, wide), 0)
    dst = lax.broadcasted_iota(jnp.int32, (4 * LAT, wide), 1)
    wanted = dst // (4 * LAT) * 2 * LAT + (dst // LAT + 1) % 2 * LAT + dst % LAT
    chosen = jnp.where(src == wanted, 1.0, 0.0).astype(jnp.bfloat16)
    lines = []
    for row in range(3):
        packed = tbuf[row]
        lines += [packed[:, : 4 * LAT], packed[:, 4 * LAT :]]
    laid = dot(jnp.concatenate(lines, axis=0).astype(jnp.bfloat16), chosen)
    spot = lax.broadcasted_iota(jnp.int32, (3 * tok, wide), 0) % cols
    piece = lax.broadcasted_iota(jnp.int32, (3 * tok, wide), 1) // LAT % 4
    before = jnp.where(spot == 0, 0.0, pltpu.roll(laid, 1, 0))
    after = jnp.where(spot == cols - 1, 0.0, pltpu.roll(laid, 3 * tok - 1, 0))
    laid = jnp.where(piece == 0, before, jnp.where(piece == 3, after, laid)).astype(jnp.bfloat16)
    near = []
    for f in range(frames):
        for pair in range(2):
            at = pair * tok + f * cols
            near.append(
                jnp.concatenate([laid[at : at + cols], laid[at + tok : at + tok + cols]], axis=1)
            )
    near = jnp.concatenate(near, axis=0)
    first[...] = dot(near, w4[2])
    for ta in (1, 0):
        first[(2 - ta) * 2 * cols :] += dot(near[: (ta + 1) * 2 * cols], w4[ta])

    def conv(row, phase):
        at = (row % 2 * 2 + phase) * ch
        return jnp.concatenate(
            [
                first[(2 * f + row // 2) * cols : (2 * f + row // 2 + 1) * cols, at : at + ch]
                for f in range(frames)
            ],
            axis=0,
        )

    cells = 4 * tok

    def folded(parts):
        whole = parts[0] + parts[1] + parts[2] + parts[3]
        return jnp.sum(whole, axis=0, keepdims=True)

    own = [conv(1 + ri, pc) for ri in range(2) for pc in range(2)]
    mean = folded(own) / cells
    square = folded([(x - mean) * (x - mean) for x in own])
    pieces = ch // 128
    rows = [x[:, 128 * i : 128 * (i + 1)] for x in (mean, square) for i in range(pieces)]
    rows.append(jnp.zeros((8 - 2 * pieces, 128), jnp.float32))
    sbuf[me] = jnp.concatenate(rows, axis=0)

    @pl.loop(1, n)
    def _(d):
        remote(sbuf.at[me], sbuf.at[me], ssend, srecv, lax.rem(me + d, n)).start()

    drain(sbuf.at[0 : n - 1], srecv)

    def grouped(x):
        high = x.astype(jnp.bfloat16).astype(jnp.float32)
        rest = x - high
        middle = rest.astype(jnp.bfloat16).astype(jnp.float32)
        pieces = [high, middle, rest - middle, jnp.zeros((13, ch), jnp.float32)]
        split = jnp.concatenate(pieces, axis=0).astype(jnp.bfloat16)
        return jnp.sum(dot(split, gmat[...]), axis=0, keepdims=True)

    means = jnp.concatenate([sbuf[:, i] for i in range(pieces)], axis=1)
    squares = jnp.concatenate([sbuf[:, pieces + i] for i in range(pieces)], axis=1)
    middle = grouped(jnp.sum(means, axis=0, keepdims=True)) / (n * span)
    apart = means - middle
    spread = jnp.sum(squares + cells * (apart * apart), axis=0, keepdims=True)
    variance = grouped(spread) / (n * span * cells)
    root = jnp.sqrt(variance + 1e-06)

    spot = lax.broadcasted_iota(jnp.int32, (tok, ch), 0) % cols

    def place(row, x0, x1):
        left = jnp.where(spot == 0, 0.0, pltpu.roll(x1, 1, 0))
        right = jnp.where(spot == cols - 1, 0.0, pltpu.roll(x0, tok - 1, 0))
        act[:, row, :, 0:ch] = left.astype(jnp.bfloat16).reshape(frames, cols, ch)
        act[:, row, :, 3 * ch :] = right.astype(jnp.bfloat16).reshape(frames, cols, ch)

    loads[4].wait()
    loads[5].wait()
    gain = gain_ref[...].reshape(1, ch)
    shift = shift_ref[...].reshape(1, ch)

    gain = gain / root

    def active(row, phase):
        y = (conv(row, phase) - middle) * gain + shift
        y = y * jax.nn.sigmoid(y)
        if row == 0:
            y = jnp.where(me > 0, y, 0.0)
        if row == 3:
            y = jnp.where(me < n - 1, y, 0.0)
        return y

    for row in range(4):
        x0 = active(row, 0)
        x1 = active(row, 1)
        act[:, row, :, ch : 2 * ch] = x0.astype(jnp.bfloat16).reshape(frames, cols, ch)
        act[:, row, :, 2 * ch : 3 * ch] = x1.astype(jnp.bfloat16).reshape(frames, cols, ch)
        place(row, x0, x1)

    weights.wait()

    def tap(ta, tb):
        rows = []
        for f in range(ta + 1):
            for pc in range(2):
                rows.append(
                    act[f, tb : tb + 2, :, pc * ch : (pc + 3) * ch].reshape(2 * cols, 3 * ch)
                )
        return dot(jnp.concatenate(rows, axis=0), wm[3 * ta + tb])

    for tb in range(3):
        for ta in (2, 1, 0):
            if tb == 0 and ta == 2:
                acc[...] = tap(ta, tb)
            else:
                acc[(2 - ta) * 4 * cols :] += tap(ta, tb)

    for f in range(frames):
        for pc in range(2):
            for ri in range(2):
                at = ((f * 2 + pc) * 2 + ri) * cols
                base = own[2 * ri + pc][f * cols : (f + 1) * cols]
                total = base + acc[at : at + cols]
                lines = pl.ds((f * 2 + ri) * 2 * cols + pc, cols, stride=2)
                for i in range(pieces):
                    woven[i, lines] = total[:, 128 * i : 128 * (i + 1)]
    for i in range(pieces):
        out_ref[:, :, :, 128 * i : 128 * (i + 1)] = (
            woven[i].reshape(frames, 2, 2 * cols, 128).astype(jnp.bfloat16)
        )

    drain(kv.at[:, 0, 0 : A - 1], zsend.at[0])
    drain(qbuf.at[:, 0 : A - 1], zsend.at[1])
    if BH > 1:
        drain(kv.at[:, 0 : BH - 1], ysend)
    drain(kv.at[:, 0:BH], csend)
    drain(part.at[0 : A - 1], lsend)
    drain(sbuf.at[0 : n - 1], ssend)

    @pl.when(me > 0)
    def _():
        drain(tbuf.at[1], tsend.at[0])

    @pl.when(me < n - 1)
    def _():
        drain(tbuf.at[1], tsend.at[1])


def shards(
    n,
    queries,
    keys,
    values,
    stream,
    head_weight,
    conv_in_weight,
    norm_gain,
    norm_shift,
    conv_mid_weight,
):
    frames, rows_here, cols, width = queries.shape
    assert frames == 3 and rows_here == 1
    tok = frames * cols
    hd = width // HEADS
    ch = norm_gain.shape[0]
    A = QUARTERS
    B = n // A
    BH = B // 2
    H = HEADS // A
    PAIRS = (H + 1) // 2
    ITEMS = H + PAIRS
    bf16, f32 = jnp.bfloat16, jnp.float32
    vmem = pl.BlockSpec(memory_space=pltpu.VMEM)
    hbm = pl.BlockSpec(memory_space=pl.ANY)
    dma = pltpu.SemaphoreType.DMA
    operands = [
        pltpu.with_memory_space_constraint(x, pltpu.HBM)
        for x in (
            queries.reshape(tok, width),
            keys.reshape(tok, width),
            values.reshape(tok, width),
            stream.reshape(tok, width),
            head_weight.T,
            conv_in_weight.reshape(9, 3 * LAT, ch),
            norm_gain,
            norm_shift,
            conv_mid_weight.reshape(9, 3 * ch, ch),
        )
    ]
    out = pl.pallas_call(
        functools.partial(body, n, frames, cols),
        out_shape=jax.ShapeDtypeStruct((frames, 2, 2 * cols, ch), bf16),
        in_specs=[hbm] * 9,
        out_specs=vmem,
        scratch_shapes=[
            pltpu.VMEM((tok, width), bf16),
            pltpu.VMEM((ch,), f32),
            pltpu.VMEM((ch,), f32),
            pltpu.VMEM((tok, width), bf16),
            pltpu.VMEM((4 * LAT, width), bf16),
            pltpu.VMEM((9, 3 * LAT, ch), bf16),
            pltpu.VMEM((A, PAIRS, tok, 8 * LAT), bf16),
            pltpu.VMEM((H, A, tok, hd), bf16),
            pltpu.VMEM((ITEMS, B, A, tok, hd), bf16),
            pltpu.VMEM((A * tok, 8 * LAT), f32),
            pltpu.VMEM((A, tok // 2, 8 * LAT), f32),
            pltpu.VMEM((A, tok // 2, 8 * LAT), f32),
            pltpu.VMEM((3, tok // 2, 8 * LAT), f32),
            pltpu.VMEM((3, 16 * LAT, 4 * ch), bf16),
            pltpu.VMEM((9, 3 * ch, ch), bf16),
            pltpu.VMEM((ch, ch), bf16),
            pltpu.VMEM((2 * tok, 4 * ch), f32),
            pltpu.VMEM((frames, 4, cols, 4 * ch), bf16),
            pltpu.VMEM((4 * tok, ch), f32),
            pltpu.VMEM((ch // 128, 4 * tok, 128), f32),
            pltpu.VMEM((n, 8, 128), f32),
            dma((2,)),
            dma((H,)),
            dma((ITEMS,)),
            dma,
            dma,
            dma((ITEMS, BH)),
            dma,
            dma((ITEMS, BH)),
            dma,
            dma,
            dma((2,)),
            dma((2,)),
            dma,
            dma,
            dma,
            dma((6,)),
        ],
        compiler_params=pltpu.CompilerParams(
            collective_id=0, has_side_effects=True, vmem_limit_bytes=44 * 2**20
        ),
        name="decode",
    )(*operands)
    return out


def solution(mesh):
    row = P("groups", "seq", None, None)
    return jax.shard_map(
        functools.partial(shards, mesh.shape["seq"]),
        mesh=mesh,
        in_specs=(row, row, row, row, P(), P(), P(), P(), P()),
        out_specs=row,
        check_vma=False,
    )
```

```python
import functools
import math

import jax
import jax.numpy as jnp
from jax import lax
from jax.experimental import pallas as pl
from jax.experimental.pallas import tpu as pltpu
from jax.sharding import PartitionSpec as P

HEADS = 20
GROUPS = 32
QUARTERS = 4
LAG = 4
WINDOW = 6
LAT = 16
NT = (((1,), (1,)), ((), ()))


def dot(a, b):
    return jnp.dot(a, b, preferred_element_type=jnp.float32)


def dot_t(a, b):
    return lax.dot_general(a, b, NT, preferred_element_type=jnp.float32)


def body(
    n,
    frames,
    cols,
    q_ref,
    k_ref,
    v_hbm,
    stream_hbm,
    head_hbm,
    wi_hbm,
    gain_hbm,
    shift_hbm,
    wm_hbm,
    out_ref,
    v_ref,
    gain_ref,
    shift_ref,
    stream_ref,
    head_ref,
    wi_ref,
    vsend,
    qbuf,
    kv,
    sums,
    part,
    lbuf,
    upart,
    ubuf,
    dpart,
    dbuf,
    pick_own,
    pick_near,
    edge,
    hbuf,
    w4,
    wm,
    gmat,
    first,
    act,
    acc,
    woven,
    sbuf,
    zsend,
    zq,
    zkv,
    loc,
    ysend,
    yrecv,
    yown,
    cown,
    ksem,
    csend,
    crecv,
    lsend,
    lrecv,
    usend,
    urecv,
    dsend,
    drecv,
    hsend,
    hrecv,
    ssend,
    srecv,
    wsem,
    isem,
):
    A = QUARTERS
    B = n // A
    BH = B // 2
    H = HEADS // A
    PAIRS = (H + 1) // 2
    ITEMS = H + PAIRS
    tok = frames * cols
    hd = q_ref.shape[1] // HEADS
    ch = gain_ref.shape[0]
    scale = math.log2(math.e) / hd**0.5
    me = lax.axis_index("seq")
    a = me // B
    b = me % B
    bh = b // 2
    core = b % 2
    sibling = me + 1 - 2 * core

    def remote(src, dst, ssem, rsem, to):
        return pltpu.make_async_remote_copy(
            src_ref=src,
            dst_ref=dst,
            send_sem=ssem,
            recv_sem=rsem,
            device_id={"seq": to},
            device_id_type=pl.DeviceIdType.MESH,
        )

    def drain(ref, sem):
        pltpu.make_async_copy(ref, ref, sem).wait()

    def columns(quarter, h):
        return pl.ds(pl.multiple_of((quarter * H + h) * hd, hd), hd)

    def key_at(h):
        return h + (h + 1) // 2

    def value_at(p):
        return 3 * p + 1

    barrier = pltpu.get_barrier_semaphore()
    partners = [lax.rem(a + d, A) * B + b for d in range(1, A)]
    partners += [a * B + lax.rem(bh + d, BH) * 2 + core for d in range(1, BH)]
    partners.append(sibling)
    for to in partners:
        pl.semaphore_signal(
            barrier, inc=1, device_id={"seq": to}, device_id_type=pl.DeviceIdType.MESH
        )

    loads = [
        pltpu.make_async_copy(src, dst, isem.at[i])
        for i, (src, dst) in enumerate(
            (
                (v_hbm, v_ref),
                (head_hbm, head_ref),
                (wi_hbm, wi_ref),
                (stream_hbm, stream_ref),
                (gain_hbm, gain_ref),
                (shift_hbm, shift_ref),
            )
        )
    ]
    for load in loads:
        load.start()
    for h in range(H):
        cut = columns(a, h)
        pltpu.make_async_copy(k_ref.at[:, cut], kv.at[key_at(h), b, 0], ksem).start()
        pltpu.make_async_copy(q_ref.at[:, cut], qbuf.at[h, a], zq.at[h]).start()

    loads[0].wait()
    loads[1].wait()
    upper = lax.broadcasted_iota(jnp.int32, (4 * LAT, 2 * hd), 1) < hd
    for quarter in range(A):
        for p in range(PAIRS):
            wide = min(2, H - 2 * p) * hd
            at = (quarter * H + 2 * p) * hd
            w = head_ref[:, at : at + wide]
            if wide > hd:
                zero = jnp.zeros_like(w)
                w = jnp.concatenate(
                    [jnp.where(upper, w, zero), jnp.where(upper, zero, w)], axis=0
                )
            else:
                w = jnp.concatenate([w, jnp.zeros_like(w)], axis=0)
            vsend[quarter, p] = dot_t(v_ref[:, at : at + wide], w).astype(jnp.bfloat16)
    for p in range(PAIRS):
        kv[value_at(p), b, 0] = vsend[a, p]

    for h in range(H):
        drain(kv.at[key_at(h), b, 0], ksem)

    pl.semaphore_wait(barrier, len(partners))

    def scatter(j):
        for d in range(1, A):
            to = lax.rem(a + d, A)
            peer = to * B + b
            if j >= ITEMS:
                h = j - ITEMS
                src = q_ref.at[:, columns(to, h)]
                remote(src, qbuf.at[h, a], zsend.at[1], zq.at[h], peer).start()
            else:
                if j % 3 == 1:
                    src = vsend.at[to, j // 3]
                else:
                    src = k_ref.at[:, columns(to, j - (j + 1) // 3)]
                remote(src, kv.at[j, b, A - d], zsend.at[0], zkv.at[j], peer).start()

    for j in range(WINDOW):
        scatter(j)

    own = kv.at[:, b, 0]
    for d in range(1, BH):
        to = a * B + lax.rem(bh + d, BH) * 2 + core
        remote(own, own, ysend, yown.at[d], to).start()
    remote(own, own, csend, cown.at[0], sibling).start()

    hbuf[...] = jnp.zeros_like(hbuf)
    weights = pltpu.make_async_copy(wm_hbm, wm, wsem)
    weights.start()

    w4[...] = jnp.zeros_like(w4)
    loads[2].wait()
    for ta in range(3):
        for ri in range(2):
            for pc in range(2):
                for tb in range(3):
                    at = (2, 0, 1, 3)[ri + tb] * 4 * LAT + LAT * pc
                    to = (2 * ri + pc) * ch
                    w4[ta, at : at + 3 * LAT, to : to + ch] = wi_ref[3 * ta + tb]
    span = ch // GROUPS

    def group_of(axis):
        at = lax.broadcasted_iota(jnp.int32, (ch, ch), axis).astype(jnp.float32)
        return jnp.floor((at + 0.5) * (1.0 / span))

    gmat[...] = jnp.where(group_of(0) == group_of(1), 1.0, 0.0).astype(jnp.bfloat16)
    def spot_of(shape, lanes):
        src = lax.broadcasted_iota(jnp.int32, shape, 0)
        dst = lax.broadcasted_iota(jnp.int32, shape, 1) % lanes
        return src, dst, (dst // LAT + 1) % 2 * LAT + dst % LAT

    lane_side = lax.broadcasted_iota(jnp.int32, (8 * LAT, 16 * LAT), 1) // (8 * LAT)
    src, dst, inner = spot_of((8 * LAT, 16 * LAT), 8 * LAT)
    wanted = lane_side * 4 * LAT + dst // (4 * LAT) * 2 * LAT + inner
    pick_own[...] = jnp.where(src == wanted, 1.0, 0.0).astype(jnp.bfloat16)
    block = lax.broadcasted_iota(jnp.int32, (16 * LAT, 24 * LAT), 1) // (8 * LAT)
    src, dst, inner = spot_of((16 * LAT, 24 * LAT), 8 * LAT)
    below = dst // (4 * LAT)
    first_at = jnp.where(below == 0, jnp.where(block == 2, 0, 1 + 2 * block), 0)
    last_at = jnp.where(below == 1, jnp.where(block == 2, 1, 2 * block), 0)
    wanted = below * 8 * LAT + (first_at + last_at) * 2 * LAT + inner
    pick_near[...] = jnp.where(src == wanted, 1.0, 0.0).astype(jnp.bfloat16)
    sums[...] = jnp.zeros_like(sums)
    ubuf[...] = jnp.zeros_like(ubuf)
    dbuf[...] = jnp.zeros_like(dbuf)
    loads[3].wait()
    streamed = dot_t(stream_ref[...], head_ref[...])
    streamed = jnp.concatenate([streamed, jnp.zeros_like(streamed)], axis=1)
    sums[pl.ds(pl.multiple_of(a * tok, 8), tok)] = streamed

    def spread_on(j):
        for d in range(1, BH):
            theirs = lax.rem(bh + BH - d, BH) * 2 + core
            slab = kv.at[j, theirs, 1:A]
            drain(slab, yrecv.at[j, d])
            remote(slab, slab, csend, crecv.at[j, d], sibling).start()

    for j in range(ITEMS):
        slab = kv.at[j, b, 1:A]
        drain(slab, zkv.at[j])
        if j + WINDOW < ITEMS + H:
            scatter(j + WINDOW)
        for d in range(1, BH):
            to = a * B + lax.rem(bh + d, BH) * 2 + core
            remote(slab, slab, ysend, yrecv.at[j, d], to).start()
        remote(slab, slab, csend, crecv.at[j, 0], sibling).start()
        if j == LAG - 1:
            for d in range(1, BH):
                theirs = lax.rem(bh + BH - d, BH) * 2 + core
                slab = kv.at[:, theirs, 0]
                drain(slab, yown.at[d])
                remote(slab, slab, csend, cown.at[d], sibling).start()
        if j >= LAG:
            spread_on(j - LAG)
    for j in range(ITEMS + WINDOW, ITEMS + H):
        scatter(j)

    def gathered(j):
        for d in range(BH):
            theirs = lax.rem(bh + BH - d, BH) * 2 + 1 - core
            drain(kv.at[j, theirs, 1:A], crecv.at[j, d])

    side = lax.broadcasted_iota(jnp.int32, (A * tok, 8 * LAT), 1) // (4 * LAT)

    late = ITEMS - LAG
    for h in range(H):
        needed = max(key_at(h), value_at(h // 2))
        while late < ITEMS and late <= max(needed, ITEMS - LAG + h):
            spread_on(late)
            late += 1
        if h == 0:
            for d in range(BH):
                theirs = lax.rem(bh + BH - d, BH) * 2 + 1 - core
                drain(kv.at[:, theirs, 0], cown.at[d])
        gathered(key_at(h))
        if h % 2 == 0:
            gathered(value_at(h // 2))
        drain(qbuf.at[h], zq.at[h])
        query = qbuf[h].reshape(A * tok, hd)
        key = kv[key_at(h)].reshape(n * tok, hd)
        value = kv[value_at(h // 2)].reshape(n * tok, 8 * LAT)
        scores = dot_t(query, key)
        top = jnp.max(scores, axis=-1, keepdims=True)
        expo = jnp.exp2((scores - top) * scale)
        total = jnp.sum(expo, axis=-1, keepdims=True)
        out = dot(expo.astype(jnp.bfloat16), value) / total
        sums[...] += jnp.where(side == h % 2, out, 0.0)

    whole = sums[...]
    whole = whole + pltpu.roll(whole, 4 * LAT, 1)
    turned = pltpu.roll(whole, 2 * LAT, 1)
    whole = whole.reshape(A, tok, 8 * LAT)
    turned = turned.reshape(A, tok, 8 * LAT)
    left = lax.broadcasted_iota(jnp.int32, (A, 2 * cols, 8 * LAT), 2) < 4 * LAT
    part[...] = jnp.where(left, whole[:, : 2 * cols], whole[:, cols:]).astype(jnp.bfloat16)
    quarter_of = lax.broadcasted_iota(jnp.int32, (A, cols, 8 * LAT), 2) // (2 * LAT)
    thirds = [whole[:, i * cols : (i + 1) * cols] for i in range(2)] + [turned[:, 2 * cols :]]
    upper = jnp.where(quarter_of == 1, thirds[0], jnp.where(quarter_of == 3, thirds[1], thirds[2]))
    lower = jnp.where(quarter_of == 0, thirds[0], jnp.where(quarter_of == 2, thirds[1], thirds[2]))
    upart[...] = upper.astype(jnp.bfloat16)
    dpart[...] = lower.astype(jnp.bfloat16)

    def near_rows(act_on):
        for d in range(A):
            z = lax.rem(a + d, A)
            row = z * B + b

            @pl.when(row < n - 1)
            def _():
                act_on(remote(upart.at[z], ubuf.at[a], usend, urecv, row + 1))

            @pl.when(row > 0)
            def _():
                act_on(remote(dpart.at[z], dbuf.at[a], dsend, drecv, row - 1))

    for d in range(1, A):
        to = lax.rem(a + d, A)
        remote(part.at[to], lbuf.at[a], lsend, lrecv, to * B + b).start()
    near_rows(lambda copy: copy.start())
    lbuf[a] = part[a]
    drain(lbuf.at[0 : A - 1], lrecv)

    @pl.when(me > 0)
    def _():
        drain(ubuf, urecv)

    @pl.when(me < n - 1)
    def _():
        drain(dbuf, drecv)

    def total_of(ref):
        total = ref[0].astype(jnp.float32)
        for d in range(1, A):
            total = total + ref[d].astype(jnp.float32)
        return total.astype(jnp.bfloat16)

    laid = dot(total_of(lbuf), pick_own[...])
    own_rows = jnp.concatenate([laid[:, : 8 * LAT], laid[cols:, 8 * LAT :]], axis=0)
    laid = dot(jnp.concatenate([total_of(ubuf), total_of(dbuf)], axis=1), pick_near[...])
    near_lines = jnp.concatenate(
        [laid[:, i * 8 * LAT : (i + 1) * 8 * LAT] for i in range(3)], axis=0
    )
    laid = jnp.concatenate([own_rows, near_lines], axis=0)
    wide = 8 * LAT
    spot = lax.broadcasted_iota(jnp.int32, (2 * tok, wide), 0) % cols
    piece = lax.broadcasted_iota(jnp.int32, (2 * tok, wide), 1) // LAT % 4
    before = jnp.where(spot == 0, 0.0, pltpu.roll(laid, 1, 0))
    after = jnp.where(spot == cols - 1, 0.0, pltpu.roll(laid, 2 * tok - 1, 0))
    laid = jnp.where(piece == 0, before, jnp.where(piece == 3, after, laid)).astype(jnp.bfloat16)
    near = jnp.concatenate([laid[:tok], laid[tok:]], axis=1)
    first[...] = dot(near, w4[2])
    for ta in (1, 0):
        first[(2 - ta) * cols :] += dot(near[: (ta + 1) * cols], w4[ta])

    edge[...] = first[...].astype(jnp.bfloat16)

    @pl.when(me > 0)
    def _():
        remote(edge.at[:, : 2 * ch], hbuf.at[1], hsend.at[0], hrecv.at[1], me - 1).start()

    @pl.when(me < n - 1)
    def _():
        remote(edge.at[:, 2 * ch :], hbuf.at[0], hsend.at[1], hrecv.at[0], me + 1).start()

    def conv(row, phase):
        if row in (1, 2):
            at = ((row - 1) * 2 + phase) * ch
            return first[:, at : at + ch]
        return hbuf[row // 3, :, phase * ch : (phase + 1) * ch].astype(jnp.float32)

    cells = 4 * tok

    def folded(parts):
        whole = parts[0] + parts[1] + parts[2] + parts[3]
        return jnp.sum(whole, axis=0, keepdims=True)

    own = [conv(1 + ri, pc) for ri in range(2) for pc in range(2)]
    mean = folded(own) / cells
    square = folded([(x - mean) * (x - mean) for x in own])
    pieces = ch // 128
    rows = [x[:, 128 * i : 128 * (i + 1)] for x in (mean, square) for i in range(pieces)]
    sbuf[me, : 2 * pieces] = jnp.concatenate(rows, axis=0)

    @pl.loop(1, n)
    def _(d):
        mine = sbuf.at[me, 0 : 2 * pieces]
        remote(mine, mine, ssend, srecv, lax.rem(me + d, n)).start()

    drain(sbuf.at[0 : n - 1, 0 : 2 * pieces], srecv)

    def grouped(x):
        high = x.astype(jnp.bfloat16).astype(jnp.float32)
        rest = x - high
        middle = rest.astype(jnp.bfloat16).astype(jnp.float32)
        pieces = [high, middle, rest - middle, jnp.zeros((13, ch), jnp.float32)]
        split = jnp.concatenate(pieces, axis=0).astype(jnp.bfloat16)
        return jnp.sum(dot(split, gmat[...]), axis=0, keepdims=True)

    means = jnp.concatenate([sbuf[:, i] for i in range(pieces)], axis=1)
    squares = jnp.concatenate([sbuf[:, pieces + i] for i in range(pieces)], axis=1)
    middle = grouped(jnp.sum(means, axis=0, keepdims=True)) / (n * span)
    apart = means - middle
    spread = jnp.sum(squares + cells * (apart * apart), axis=0, keepdims=True)
    variance = grouped(spread) / (n * span * cells)
    root = jnp.sqrt(variance + 1e-06)

    spot = lax.broadcasted_iota(jnp.int32, (tok, ch), 0) % cols

    def place(row, x0, x1):
        left = jnp.where(spot == 0, 0.0, pltpu.roll(x1, 1, 0))
        right = jnp.where(spot == cols - 1, 0.0, pltpu.roll(x0, tok - 1, 0))
        act[:, row, :, 0:ch] = left.astype(jnp.bfloat16).reshape(frames, cols, ch)
        act[:, row, :, 3 * ch :] = right.astype(jnp.bfloat16).reshape(frames, cols, ch)

    loads[4].wait()
    loads[5].wait()
    gain = gain_ref[...].reshape(1, ch)
    shift = shift_ref[...].reshape(1, ch)

    gain = gain / root

    def active(row, phase):
        y = (conv(row, phase) - middle) * gain + shift
        y = y * jax.nn.sigmoid(y)
        if row == 0:
            y = jnp.where(me > 0, y, 0.0)
        if row == 3:
            y = jnp.where(me < n - 1, y, 0.0)
        return y

    @pl.when(me > 0)
    def _():
        drain(hbuf.at[0], hrecv.at[0])

    @pl.when(me < n - 1)
    def _():
        drain(hbuf.at[1], hrecv.at[1])

    for row in (1, 2, 0, 3):
        x0 = active(row, 0)
        x1 = active(row, 1)
        act[:, row, :, ch : 2 * ch] = x0.astype(jnp.bfloat16).reshape(frames, cols, ch)
        act[:, row, :, 2 * ch : 3 * ch] = x1.astype(jnp.bfloat16).reshape(frames, cols, ch)
        place(row, x0, x1)

    weights.wait()

    def tap(ta, tb):
        rows = []
        for f in range(ta + 1):
            for pc in range(2):
                rows.append(
                    act[f, tb : tb + 2, :, pc * ch : (pc + 3) * ch].reshape(2 * cols, 3 * ch)
                )
        return dot(jnp.concatenate(rows, axis=0), wm[3 * ta + tb])

    for tb in range(3):
        for ta in (2, 1, 0):
            if tb == 0 and ta == 2:
                acc[...] = tap(ta, tb)
            else:
                acc[(2 - ta) * 4 * cols :] += tap(ta, tb)

    for f in range(frames):
        for pc in range(2):
            for ri in range(2):
                at = ((f * 2 + pc) * 2 + ri) * cols
                base = own[2 * ri + pc][f * cols : (f + 1) * cols]
                total = base + acc[at : at + cols]
                lines = pl.ds((f * 2 + ri) * 2 * cols + pc, cols, stride=2)
                for i in range(pieces):
                    woven[i, lines] = total[:, 128 * i : 128 * (i + 1)]
    for i in range(pieces):
        out_ref[:, :, :, 128 * i : 128 * (i + 1)] = (
            woven[i].reshape(frames, 2, 2 * cols, 128).astype(jnp.bfloat16)
        )

    drain(kv.at[:, 0, 0 : A - 1], zsend.at[0])
    drain(qbuf.at[:, 0 : A - 1], zsend.at[1])
    if BH > 1:
        drain(kv.at[:, 0 : BH - 1], ysend)
    drain(kv.at[:, 0:BH], csend)
    drain(part.at[0 : A - 1], lsend)
    drain(sbuf.at[0 : n - 1, 0 : 2 * pieces], ssend)

    near_rows(lambda copy: copy.wait_send())

    @pl.when(me > 0)
    def _():
        drain(hbuf.at[0], hsend.at[0])

    @pl.when(me < n - 1)
    def _():
        drain(hbuf.at[1], hsend.at[1])


def shards(
    n,
    queries,
    keys,
    values,
    stream,
    head_weight,
    conv_in_weight,
    norm_gain,
    norm_shift,
    conv_mid_weight,
):
    frames, rows_here, cols, width = queries.shape
    assert frames == 3 and rows_here == 1
    tok = frames * cols
    hd = width // HEADS
    ch = norm_gain.shape[0]
    A = QUARTERS
    B = n // A
    BH = B // 2
    H = HEADS // A
    PAIRS = (H + 1) // 2
    ITEMS = H + PAIRS
    bf16, f32 = jnp.bfloat16, jnp.float32
    vmem = pl.BlockSpec(memory_space=pltpu.VMEM)
    hbm = pl.BlockSpec(memory_space=pl.ANY)
    dma = pltpu.SemaphoreType.DMA
    operands = [
        pltpu.with_memory_space_constraint(x, pltpu.HBM)
        for x in (
            queries.reshape(tok, width),
            keys.reshape(tok, width),
            values.reshape(tok, width),
            stream.reshape(tok, width),
            head_weight.T,
            conv_in_weight.reshape(9, 3 * LAT, ch),
            norm_gain,
            norm_shift,
            conv_mid_weight.reshape(9, 3 * ch, ch),
        )
    ]
    out = pl.pallas_call(
        functools.partial(body, n, frames, cols),
        out_shape=jax.ShapeDtypeStruct((frames, 2, 2 * cols, ch), bf16),
        in_specs=[hbm] * 9,
        out_specs=vmem,
        scratch_shapes=[
            pltpu.VMEM((tok, width), bf16),
            pltpu.VMEM((ch,), f32),
            pltpu.VMEM((ch,), f32),
            pltpu.VMEM((tok, width), bf16),
            pltpu.VMEM((4 * LAT, width), bf16),
            pltpu.VMEM((9, 3 * LAT, ch), bf16),
            pltpu.VMEM((A, PAIRS, tok, 8 * LAT), bf16),
            pltpu.VMEM((H, A, tok, hd), bf16),
            pltpu.VMEM((ITEMS, B, A, tok, hd), bf16),
            pltpu.VMEM((A * tok, 8 * LAT), f32),
            pltpu.VMEM((A, 2 * cols, 8 * LAT), bf16),
            pltpu.VMEM((A, 2 * cols, 8 * LAT), bf16),
            pltpu.VMEM((A, cols, 8 * LAT), bf16),
            pltpu.VMEM((A, cols, 8 * LAT), bf16),
            pltpu.VMEM((A, cols, 8 * LAT), bf16),
            pltpu.VMEM((A, cols, 8 * LAT), bf16),
            pltpu.VMEM((8 * LAT, 16 * LAT), bf16),
            pltpu.VMEM((16 * LAT, 24 * LAT), bf16),
            pltpu.VMEM((tok, 4 * ch), bf16),
            pltpu.VMEM((2, tok, 2 * ch), bf16),
            pltpu.VMEM((3, 16 * LAT, 4 * ch), bf16),
            pltpu.VMEM((9, 3 * ch, ch), bf16),
            pltpu.VMEM((ch, ch), bf16),
            pltpu.VMEM((tok, 4 * ch), f32),
            pltpu.VMEM((frames, 4, cols, 4 * ch), bf16),
            pltpu.VMEM((4 * tok, ch), f32),
            pltpu.VMEM((ch // 128, 4 * tok, 128), f32),
            pltpu.VMEM((n, 8, 128), f32),
            dma((2,)),
            dma((H,)),
            dma((ITEMS,)),
            dma,
            dma,
            dma((ITEMS, BH)),
            dma((BH,)),
            dma((BH,)),
            dma,
            dma,
            dma((ITEMS, BH)),
            dma,
            dma,
            dma,
            dma,
            dma,
            dma,
            dma((2,)),
            dma((2,)),
            dma,
            dma,
            dma,
            dma((6,)),
        ],
        compiler_params=pltpu.CompilerParams(
            collective_id=0, has_side_effects=True, vmem_limit_bytes=44 * 2**20
        ),
        name="decode",
    )(*operands)
    return out


def solution(mesh):
    row = P("groups", "seq", None, None)
    return jax.shard_map(
        functools.partial(shards, mesh.shape["seq"]),
        mesh=mesh,
        in_specs=(row, row, row, row, P(), P(), P(), P(), P()),
        out_specs=row,
        check_vma=False,
    )
```

```python
import functools
import math

import jax
import jax.numpy as jnp
from jax import lax
from jax.experimental import pallas as pl
from jax.experimental.pallas import tpu as pltpu
from jax.sharding import PartitionSpec as P

HEADS = 20
GROUPS = 32
QUARTERS = 4
LAG = 4
WINDOW = 6
LAT = 16
NT = (((1,), (1,)), ((), ()))


def dot(a, b):
    return jnp.dot(a, b, preferred_element_type=jnp.float32)


def dot_t(a, b):
    return lax.dot_general(a, b, NT, preferred_element_type=jnp.float32)


def body(
    n,
    frames,
    cols,
    q_ref,
    k_ref,
    v_hbm,
    stream_hbm,
    head_hbm,
    wi_hbm,
    gain_hbm,
    shift_hbm,
    wm_hbm,
    out_ref,
    v_ref,
    gain_ref,
    shift_ref,
    stream_ref,
    head_ref,
    wi_ref,
    vsend,
    qbuf,
    kv,
    sums,
    part,
    lbuf,
    upart,
    ubuf,
    dpart,
    dbuf,
    pick_own,
    pick_near,
    edge,
    hbuf,
    w4,
    wm,
    gmat,
    first,
    act,
    acc,
    woven,
    sbuf,
    zsend,
    zq,
    zkv,
    loc,
    ysend,
    yrecv,
    yown,
    cown,
    ksem,
    csend,
    crecv,
    lsend,
    lrecv,
    usend,
    urecv,
    dsend,
    drecv,
    hsend,
    hrecv,
    ssend,
    srecv,
    wsem,
    isem,
):
    A = QUARTERS
    B = n // A
    BH = B // 2
    H = HEADS // A
    PAIRS = (H + 1) // 2
    ITEMS = H + PAIRS
    tok = frames * cols
    hd = q_ref.shape[1] // HEADS
    ch = gain_ref.shape[0]
    scale = math.log2(math.e) / hd**0.5
    me = lax.axis_index("seq")
    a = me // B
    b = me % B
    bh = b // 2
    core = b % 2
    sibling = me + 1 - 2 * core

    def remote(src, dst, ssem, rsem, to):
        return pltpu.make_async_remote_copy(
            src_ref=src,
            dst_ref=dst,
            send_sem=ssem,
            recv_sem=rsem,
            device_id={"seq": to},
            device_id_type=pl.DeviceIdType.MESH,
        )

    def drain(ref, sem):
        pltpu.make_async_copy(ref, ref, sem).wait()

    def columns(quarter, h):
        return pl.ds(pl.multiple_of((quarter * H + h) * hd, hd), hd)

    def key_at(h):
        return h + (h + 1) // 2

    def value_at(p):
        return 3 * p + 1

    barrier = pltpu.get_barrier_semaphore()
    partners = [lax.rem(a + d, A) * B + b for d in range(1, A)]
    partners += [a * B + lax.rem(bh + d, BH) * 2 + core for d in range(1, BH)]
    partners.append(sibling)
    for to in partners:
        pl.semaphore_signal(
            barrier, inc=1, device_id={"seq": to}, device_id_type=pl.DeviceIdType.MESH
        )

    loads = [
        pltpu.make_async_copy(src, dst, isem.at[i])
        for i, (src, dst) in enumerate(
            (
                (v_hbm, v_ref),
                (head_hbm, head_ref),
                (wi_hbm, wi_ref),
                (stream_hbm, stream_ref),
                (gain_hbm, gain_ref),
                (shift_hbm, shift_ref),
            )
        )
    ]
    for load in loads:
        load.start()
    for h in range(H):
        cut = columns(a, h)
        pltpu.make_async_copy(k_ref.at[:, cut], kv.at[key_at(h), b, 0], ksem).start()
        pltpu.make_async_copy(q_ref.at[:, cut], qbuf.at[h, a], zq.at[h]).start()

    loads[0].wait()
    loads[1].wait()
    upper = lax.broadcasted_iota(jnp.int32, (4 * LAT, 2 * hd), 1) < hd
    for quarter in range(A):
        for p in range(PAIRS):
            wide = min(2, H - 2 * p) * hd
            at = (quarter * H + 2 * p) * hd
            w = head_ref[:, at : at + wide]
            if wide > hd:
                zero = jnp.zeros_like(w)
                w = jnp.concatenate(
                    [jnp.where(upper, w, zero), jnp.where(upper, zero, w)], axis=0
                )
            else:
                w = jnp.concatenate([w, jnp.zeros_like(w)], axis=0)
            vsend[quarter, p] = dot_t(v_ref[:, at : at + wide], w).astype(jnp.bfloat16)
    for p in range(PAIRS):
        kv[value_at(p), b, 0] = vsend[a, p]

    for h in range(H):
        drain(kv.at[key_at(h), b, 0], ksem)

    pl.semaphore_wait(barrier, len(partners))

    def scatter(j):
        for d in range(1, A):
            to = lax.rem(a + d, A)
            peer = to * B + b
            if j >= ITEMS:
                h = j - ITEMS
                src = q_ref.at[:, columns(to, h)]
                remote(src, qbuf.at[h, a], zsend.at[1], zq.at[h], peer).start()
            else:
                if j % 3 == 1:
                    src = vsend.at[to, j // 3]
                else:
                    src = k_ref.at[:, columns(to, j - (j + 1) // 3)]
                remote(src, kv.at[j, b, A - d], zsend.at[0], zkv.at[j], peer).start()

    for j in range(WINDOW):
        scatter(j)

    own = kv.at[:, b, 0]
    for d in range(1, BH):
        to = a * B + lax.rem(bh + d, BH) * 2 + core
        remote(own, own, ysend, yown.at[d], to).start()
    remote(own, own, csend, cown.at[0], sibling).start()

    hbuf[...] = jnp.zeros_like(hbuf)
    weights = pltpu.make_async_copy(wm_hbm, wm, wsem)
    weights.start()

    w4[...] = jnp.zeros_like(w4)
    loads[2].wait()
    for ta in range(3):
        for ri in range(2):
            for pc in range(2):
                for tb in range(3):
                    at = (2, 0, 1, 3)[ri + tb] * 4 * LAT + LAT * pc
                    to = (2 * ri + pc) * ch
                    w4[ta, at : at + 3 * LAT, to : to + ch] = wi_ref[3 * ta + tb]
    span = ch // GROUPS

    def group_of(axis):
        at = lax.broadcasted_iota(jnp.int32, (ch, ch), axis).astype(jnp.float32)
        return jnp.floor((at + 0.5) * (1.0 / span))

    gmat[...] = jnp.where(group_of(0) == group_of(1), 1.0, 0.0).astype(jnp.bfloat16)
    def spot_of(shape, lanes):
        src = lax.broadcasted_iota(jnp.int32, shape, 0)
        dst = lax.broadcasted_iota(jnp.int32, shape, 1) % lanes
        return src, dst, (dst // LAT + 1) % 2 * LAT + dst % LAT

    lane_side = lax.broadcasted_iota(jnp.int32, (8 * LAT, 16 * LAT), 1) // (8 * LAT)
    src, dst, inner = spot_of((8 * LAT, 16 * LAT), 8 * LAT)
    wanted = lane_side * 4 * LAT + dst // (4 * LAT) * 2 * LAT + inner
    pick_own[...] = jnp.where(src == wanted, 1.0, 0.0).astype(jnp.bfloat16)
    block = lax.broadcasted_iota(jnp.int32, (16 * LAT, 24 * LAT), 1) // (8 * LAT)
    src, dst, inner = spot_of((16 * LAT, 24 * LAT), 8 * LAT)
    below = dst // (4 * LAT)
    first_at = jnp.where(below == 0, jnp.where(block == 2, 0, 1 + 2 * block), 0)
    last_at = jnp.where(below == 1, jnp.where(block == 2, 1, 2 * block), 0)
    wanted = below * 8 * LAT + (first_at + last_at) * 2 * LAT + inner
    pick_near[...] = jnp.where(src == wanted, 1.0, 0.0).astype(jnp.bfloat16)
    sums[...] = jnp.zeros_like(sums)
    ubuf[...] = jnp.zeros_like(ubuf)
    dbuf[...] = jnp.zeros_like(dbuf)
    loads[3].wait()
    streamed = dot_t(stream_ref[...], head_ref[...])
    streamed = jnp.concatenate([streamed, jnp.zeros_like(streamed)], axis=1)
    sums[pl.ds(pl.multiple_of(a * tok, 8), tok)] = streamed

    def spread_on(j):
        for d in range(1, BH):
            theirs = lax.rem(bh + BH - d, BH) * 2 + core
            slab = kv.at[j, theirs, 1:A]
            drain(slab, yrecv.at[j, d])
            remote(slab, slab, csend, crecv.at[j, d], sibling).start()

    for j in range(ITEMS):
        slab = kv.at[j, b, 1:A]
        drain(slab, zkv.at[j])
        if j + WINDOW < ITEMS + H:
            scatter(j + WINDOW)
        for d in range(1, BH):
            to = a * B + lax.rem(bh + d, BH) * 2 + core
            remote(slab, slab, ysend, yrecv.at[j, d], to).start()
        remote(slab, slab, csend, crecv.at[j, 0], sibling).start()
        if j == LAG - 1:
            for d in range(1, BH):
                theirs = lax.rem(bh + BH - d, BH) * 2 + core
                slab = kv.at[:, theirs, 0]
                drain(slab, yown.at[d])
                remote(slab, slab, csend, cown.at[d], sibling).start()
        if j >= LAG:
            spread_on(j - LAG)
    for j in range(ITEMS + WINDOW, ITEMS + H):
        scatter(j)

    def gathered(j):
        for d in range(BH):
            theirs = lax.rem(bh + BH - d, BH) * 2 + 1 - core
            drain(kv.at[j, theirs, 1:A], crecv.at[j, d])

    side = lax.broadcasted_iota(jnp.int32, (A * tok, 8 * LAT), 1) // (4 * LAT)

    late = ITEMS - LAG
    for h in range(H):
        needed = max(key_at(h), value_at(h // 2))
        while late < ITEMS and late <= max(needed, ITEMS - LAG + h):
            spread_on(late)
            late += 1
        if h == 0:
            for d in range(BH):
                theirs = lax.rem(bh + BH - d, BH) * 2 + 1 - core
                drain(kv.at[:, theirs, 0], cown.at[d])
        gathered(key_at(h))
        if h % 2 == 0:
            gathered(value_at(h // 2))
        drain(qbuf.at[h], zq.at[h])
        query = qbuf[h].reshape(A * tok, hd)
        key = kv[key_at(h)].reshape(n * tok, hd)
        value = kv[value_at(h // 2)].reshape(n * tok, 8 * LAT)
        scores = dot_t(query, key)
        top = jnp.max(scores, axis=-1, keepdims=True)
        expo = jnp.exp2((scores - top) * scale)
        total = jnp.sum(expo, axis=-1, keepdims=True)
        out = dot(expo.astype(jnp.bfloat16), value) / total
        sums[...] += jnp.where(side == h % 2, out, 0.0)

    whole = sums[...]
    whole = whole + pltpu.roll(whole, 4 * LAT, 1)
    turned = pltpu.roll(whole, 2 * LAT, 1)
    whole = whole.reshape(A, tok, 8 * LAT)
    turned = turned.reshape(A, tok, 8 * LAT)
    left = lax.broadcasted_iota(jnp.int32, (A, 2 * cols, 8 * LAT), 2) < 4 * LAT
    part[...] = jnp.where(left, whole[:, : 2 * cols], whole[:, cols:]).astype(jnp.bfloat16)
    quarter_of = lax.broadcasted_iota(jnp.int32, (A, cols, 8 * LAT), 2) // (2 * LAT)
    thirds = [whole[:, i * cols : (i + 1) * cols] for i in range(2)] + [turned[:, 2 * cols :]]
    upper = jnp.where(quarter_of == 1, thirds[0], jnp.where(quarter_of == 3, thirds[1], thirds[2]))
    lower = jnp.where(quarter_of == 0, thirds[0], jnp.where(quarter_of == 2, thirds[1], thirds[2]))
    upart[...] = upper.astype(jnp.bfloat16)
    dpart[...] = lower.astype(jnp.bfloat16)

    def near_rows(act_on):
        for d in range(A):
            z = lax.rem(a + d, A)
            row = z * B + b

            @pl.when(row < n - 1)
            def _():
                act_on(remote(upart.at[z], ubuf.at[a], usend, urecv, row + 1))

            @pl.when(row > 0)
            def _():
                act_on(remote(dpart.at[z], dbuf.at[a], dsend, drecv, row - 1))

    for d in range(1, A):
        to = lax.rem(a + d, A)
        remote(part.at[to], lbuf.at[a], lsend, lrecv, to * B + b).start()
    near_rows(lambda copy: copy.start())
    lbuf[a] = part[a]
    drain(lbuf.at[0 : A - 1], lrecv)

    @pl.when(me > 0)
    def _():
        drain(ubuf, urecv)

    @pl.when(me < n - 1)
    def _():
        drain(dbuf, drecv)

    def total_of(ref):
        total = ref[0].astype(jnp.float32)
        for d in range(1, A):
            total = total + ref[d].astype(jnp.float32)
        return total.astype(jnp.bfloat16)

    laid = dot(total_of(lbuf), pick_own[...])
    own_rows = jnp.concatenate([laid[:, : 8 * LAT], laid[cols:, 8 * LAT :]], axis=0)
    laid = dot(jnp.concatenate([total_of(ubuf), total_of(dbuf)], axis=1), pick_near[...])
    near_lines = jnp.concatenate(
        [laid[:, i * 8 * LAT : (i + 1) * 8 * LAT] for i in range(3)], axis=0
    )
    laid = jnp.concatenate([own_rows, near_lines], axis=0)
    wide = 8 * LAT
    spot = lax.broadcasted_iota(jnp.int32, (2 * tok, wide), 0) % cols
    piece = lax.broadcasted_iota(jnp.int32, (2 * tok, wide), 1) // LAT % 4
    before = jnp.where(spot == 0, 0.0, pltpu.roll(laid, 1, 0))
    after = jnp.where(spot == cols - 1, 0.0, pltpu.roll(laid, 2 * tok - 1, 0))
    laid = jnp.where(piece == 0, before, jnp.where(piece == 3, after, laid)).astype(jnp.bfloat16)
    near = jnp.concatenate([laid[:tok], laid[tok:]], axis=1)
    first[...] = dot(near, w4[2])
    for ta in (1, 0):
        first[(2 - ta) * cols :] += dot(near[: (ta + 1) * cols], w4[ta])

    edge[...] = first[...].astype(jnp.bfloat16)

    def conv(row, phase):
        if row in (1, 2):
            at = ((row - 1) * 2 + phase) * ch
            return first[:, at : at + ch]
        return hbuf[row // 3, :, phase * ch : (phase + 1) * ch].astype(jnp.float32)

    cells = 4 * tok

    def folded(parts):
        whole = parts[0] + parts[1] + parts[2] + parts[3]
        return jnp.sum(whole, axis=0, keepdims=True)

    own = [conv(1 + ri, pc) for ri in range(2) for pc in range(2)]
    mean = folded(own) / cells
    square = folded([(x - mean) * (x - mean) for x in own])
    pieces = ch // 128
    rows = [x[:, 128 * i : 128 * (i + 1)] for x in (mean, square) for i in range(pieces)]
    sbuf[me, : 2 * pieces] = jnp.concatenate(rows, axis=0)

    @pl.loop(1, n)
    def _(d):
        mine = sbuf.at[me, 0 : 2 * pieces]
        remote(mine, mine, ssend, srecv, lax.rem(me + d, n)).start()

    @pl.when(me > 0)
    def _():
        remote(edge.at[:, : 2 * ch], hbuf.at[1], hsend.at[0], hrecv.at[1], me - 1).start()

    @pl.when(me < n - 1)
    def _():
        remote(edge.at[:, 2 * ch :], hbuf.at[0], hsend.at[1], hrecv.at[0], me + 1).start()

    drain(sbuf.at[0 : n - 1, 0 : 2 * pieces], srecv)

    def grouped(x):
        high = x.astype(jnp.bfloat16).astype(jnp.float32)
        rest = x - high
        middle = rest.astype(jnp.bfloat16).astype(jnp.float32)
        pieces = [high, middle, rest - middle, jnp.zeros((13, ch), jnp.float32)]
        split = jnp.concatenate(pieces, axis=0).astype(jnp.bfloat16)
        return jnp.sum(dot(split, gmat[...]), axis=0, keepdims=True)

    means = jnp.concatenate([sbuf[:, i] for i in range(pieces)], axis=1)
    squares = jnp.concatenate([sbuf[:, pieces + i] for i in range(pieces)], axis=1)
    middle = grouped(jnp.sum(means, axis=0, keepdims=True)) / (n * span)
    apart = means - middle
    spread = jnp.sum(squares + cells * (apart * apart), axis=0, keepdims=True)
    variance = grouped(spread) / (n * span * cells)
    root = jnp.sqrt(variance + 1e-06)

    spot = lax.broadcasted_iota(jnp.int32, (tok, ch), 0) % cols

    def place(row, x0, x1):
        left = jnp.where(spot == 0, 0.0, pltpu.roll(x1, 1, 0))
        right = jnp.where(spot == cols - 1, 0.0, pltpu.roll(x0, tok - 1, 0))
        act[:, row, :, 0:ch] = left.astype(jnp.bfloat16).reshape(frames, cols, ch)
        act[:, row, :, 3 * ch :] = right.astype(jnp.bfloat16).reshape(frames, cols, ch)

    loads[4].wait()
    loads[5].wait()
    gain = gain_ref[...].reshape(1, ch)
    shift = shift_ref[...].reshape(1, ch)

    gain = gain / root

    def active(row, phase):
        y = (conv(row, phase) - middle) * gain + shift
        y = y * jax.nn.sigmoid(y)
        if row == 0:
            y = jnp.where(me > 0, y, 0.0)
        if row == 3:
            y = jnp.where(me < n - 1, y, 0.0)
        return y

    def prepare(row):
        x0 = active(row, 0)
        x1 = active(row, 1)
        act[:, row, :, ch : 2 * ch] = x0.astype(jnp.bfloat16).reshape(frames, cols, ch)
        act[:, row, :, 2 * ch : 3 * ch] = x1.astype(jnp.bfloat16).reshape(frames, cols, ch)
        place(row, x0, x1)

    def tap(ta, tb):
        rows = []
        for f in range(ta + 1):
            for pc in range(2):
                rows.append(
                    act[f, tb : tb + 2, :, pc * ch : (pc + 3) * ch].reshape(2 * cols, 3 * ch)
                )
        return dot(jnp.concatenate(rows, axis=0), wm[3 * ta + tb])

    def taps(tb):
        for ta in (2, 1, 0):
            if tb == 1 and ta == 2:
                acc[...] = tap(ta, tb)
            else:
                acc[(2 - ta) * 4 * cols :] += tap(ta, tb)

    prepare(1)
    prepare(2)
    weights.wait()
    taps(1)

    @pl.when(me > 0)
    def _():
        drain(hbuf.at[0], hrecv.at[0])

    @pl.when(me < n - 1)
    def _():
        drain(hbuf.at[1], hrecv.at[1])

    prepare(0)
    prepare(3)
    taps(0)
    taps(2)

    for f in range(frames):
        for pc in range(2):
            for ri in range(2):
                at = ((f * 2 + pc) * 2 + ri) * cols
                base = own[2 * ri + pc][f * cols : (f + 1) * cols]
                total = base + acc[at : at + cols]
                lines = pl.ds((f * 2 + ri) * 2 * cols + pc, cols, stride=2)
                for i in range(pieces):
                    woven[i, lines] = total[:, 128 * i : 128 * (i + 1)]
    for i in range(pieces):
        out_ref[:, :, :, 128 * i : 128 * (i + 1)] = (
            woven[i].reshape(frames, 2, 2 * cols, 128).astype(jnp.bfloat16)
        )

    drain(kv.at[:, 0, 0 : A - 1], zsend.at[0])
    drain(qbuf.at[:, 0 : A - 1], zsend.at[1])
    if BH > 1:
        drain(kv.at[:, 0 : BH - 1], ysend)
    drain(kv.at[:, 0:BH], csend)
    drain(part.at[0 : A - 1], lsend)
    drain(sbuf.at[0 : n - 1, 0 : 2 * pieces], ssend)

    near_rows(lambda copy: copy.wait_send())

    @pl.when(me > 0)
    def _():
        drain(hbuf.at[0], hsend.at[0])

    @pl.when(me < n - 1)
    def _():
        drain(hbuf.at[1], hsend.at[1])


def shards(
    n,
    queries,
    keys,
    values,
    stream,
    head_weight,
    conv_in_weight,
    norm_gain,
    norm_shift,
    conv_mid_weight,
):
    frames, rows_here, cols, width = queries.shape
    assert frames == 3 and rows_here == 1
    tok = frames * cols
    hd = width // HEADS
    ch = norm_gain.shape[0]
    A = QUARTERS
    B = n // A
    BH = B // 2
    H = HEADS // A
    PAIRS = (H + 1) // 2
    ITEMS = H + PAIRS
    bf16, f32 = jnp.bfloat16, jnp.float32
    vmem = pl.BlockSpec(memory_space=pltpu.VMEM)
    hbm = pl.BlockSpec(memory_space=pl.ANY)
    dma = pltpu.SemaphoreType.DMA
    operands = [
        pltpu.with_memory_space_constraint(x, pltpu.HBM)
        for x in (
            queries.reshape(tok, width),
            keys.reshape(tok, width),
            values.reshape(tok, width),
            stream.reshape(tok, width),
            head_weight.T,
            conv_in_weight.reshape(9, 3 * LAT, ch),
            norm_gain,
            norm_shift,
            conv_mid_weight.reshape(9, 3 * ch, ch),
        )
    ]
    out = pl.pallas_call(
        functools.partial(body, n, frames, cols),
        out_shape=jax.ShapeDtypeStruct((frames, 2, 2 * cols, ch), bf16),
        in_specs=[hbm] * 9,
        out_specs=vmem,
        scratch_shapes=[
            pltpu.VMEM((tok, width), bf16),
            pltpu.VMEM((ch,), f32),
            pltpu.VMEM((ch,), f32),
            pltpu.VMEM((tok, width), bf16),
            pltpu.VMEM((4 * LAT, width), bf16),
            pltpu.VMEM((9, 3 * LAT, ch), bf16),
            pltpu.VMEM((A, PAIRS, tok, 8 * LAT), bf16),
            pltpu.VMEM((H, A, tok, hd), bf16),
            pltpu.VMEM((ITEMS, B, A, tok, hd), bf16),
            pltpu.VMEM((A * tok, 8 * LAT), f32),
            pltpu.VMEM((A, 2 * cols, 8 * LAT), bf16),
            pltpu.VMEM((A, 2 * cols, 8 * LAT), bf16),
            pltpu.VMEM((A, cols, 8 * LAT), bf16),
            pltpu.VMEM((A, cols, 8 * LAT), bf16),
            pltpu.VMEM((A, cols, 8 * LAT), bf16),
            pltpu.VMEM((A, cols, 8 * LAT), bf16),
            pltpu.VMEM((8 * LAT, 16 * LAT), bf16),
            pltpu.VMEM((16 * LAT, 24 * LAT), bf16),
            pltpu.VMEM((tok, 4 * ch), bf16),
            pltpu.VMEM((2, tok, 2 * ch), bf16),
            pltpu.VMEM((3, 16 * LAT, 4 * ch), bf16),
            pltpu.VMEM((9, 3 * ch, ch), bf16),
            pltpu.VMEM((ch, ch), bf16),
            pltpu.VMEM((tok, 4 * ch), f32),
            pltpu.VMEM((frames, 4, cols, 4 * ch), bf16),
            pltpu.VMEM((4 * tok, ch), f32),
            pltpu.VMEM((ch // 128, 4 * tok, 128), f32),
            pltpu.VMEM((n, 8, 128), f32),
            dma((2,)),
            dma((H,)),
            dma((ITEMS,)),
            dma,
            dma,
            dma((ITEMS, BH)),
            dma((BH,)),
            dma((BH,)),
            dma,
            dma,
            dma((ITEMS, BH)),
            dma,
            dma,
            dma,
            dma,
            dma,
            dma,
            dma((2,)),
            dma((2,)),
            dma,
            dma,
            dma,
            dma((6,)),
        ],
        compiler_params=pltpu.CompilerParams(
            collective_id=0, has_side_effects=True, vmem_limit_bytes=44 * 2**20
        ),
        name="decode",
    )(*operands)
    return out


def solution(mesh):
    row = P("groups", "seq", None, None)
    return jax.shard_map(
        functools.partial(shards, mesh.shape["seq"]),
        mesh=mesh,
        in_specs=(row, row, row, row, P(), P(), P(), P(), P()),
        out_specs=row,
        check_vma=False,
    )
```

```python
import functools
import math

import jax
import jax.numpy as jnp
from jax import lax
from jax.experimental import pallas as pl
from jax.experimental.pallas import tpu as pltpu
from jax.sharding import PartitionSpec as P

HEADS = 20
GROUPS = 32
QUARTERS = 4
BEFORE = (4, 5, 6, 7, 7)
LAG = 4
WINDOW = 7
LAT = 16
NT = (((1,), (1,)), ((), ()))


def dot(a, b):
    return jnp.dot(a, b, preferred_element_type=jnp.float32)


def dot_t(a, b):
    return lax.dot_general(a, b, NT, preferred_element_type=jnp.float32)


def body(
    n,
    frames,
    cols,
    q_ref,
    k_ref,
    v_hbm,
    stream_hbm,
    head_hbm,
    wi_hbm,
    gain_hbm,
    shift_hbm,
    wm_hbm,
    out_ref,
    v_ref,
    gain_ref,
    shift_ref,
    stream_ref,
    head_ref,
    wi_ref,
    vsend,
    qbuf,
    kv,
    sums,
    part,
    lbuf,
    upart,
    ubuf,
    dpart,
    dbuf,
    pick_own,
    pick_near,
    edge,
    hbuf,
    held,
    w4,
    wm,
    gmat,
    first,
    act,
    acc,
    woven,
    sbuf,
    zsend,
    zq,
    zkv,
    loc,
    ysend,
    yrecv,
    yown,
    cown,
    ksem,
    csend,
    crecv,
    lsend,
    lrecv,
    usend,
    urecv,
    dsend,
    drecv,
    hsend,
    hrecv,
    ssend,
    srecv,
    wsem,
    isem,
):
    A = QUARTERS
    B = n // A
    BH = B // 2
    H = HEADS // A
    PAIRS = (H + 1) // 2
    ITEMS = H + PAIRS
    tok = frames * cols
    hd = q_ref.shape[1] // HEADS
    ch = gain_ref.shape[0]
    scale = math.log2(math.e) / hd**0.5
    me = lax.axis_index("seq")
    a = me // B
    b = me % B
    bh = b // 2
    core = b % 2
    sibling = me + 1 - 2 * core

    def remote(src, dst, ssem, rsem, to):
        return pltpu.make_async_remote_copy(
            src_ref=src,
            dst_ref=dst,
            send_sem=ssem,
            recv_sem=rsem,
            device_id={"seq": to},
            device_id_type=pl.DeviceIdType.MESH,
        )

    def drain(ref, sem):
        pltpu.make_async_copy(ref, ref, sem).wait()

    def columns(quarter, h):
        return pl.ds(pl.multiple_of((quarter * H + h) * hd, hd), hd)

    def key_at(h):
        return h + (h + 1) // 2

    def value_at(p):
        return 3 * p + 1

    low = (A - 1 - a) // (A - 1)
    high = a // (A - 1)
    far_first = [2 + low - high, 3 - high - low, 1 + 2 * high]
    barrier = pltpu.get_barrier_semaphore()
    partners = [lax.rem(a + d, A) * B + b for d in range(1, A)]
    partners += [a * B + lax.rem(bh + d, BH) * 2 + core for d in range(1, BH)]
    partners.append(sibling)
    for to in partners:
        pl.semaphore_signal(
            barrier, inc=1, device_id={"seq": to}, device_id_type=pl.DeviceIdType.MESH
        )

    loads = [
        pltpu.make_async_copy(src, dst, isem.at[i])
        for i, (src, dst) in enumerate(
            (
                (v_hbm, v_ref),
                (head_hbm, head_ref),
                (wi_hbm, wi_ref),
                (stream_hbm, stream_ref),
                (gain_hbm, gain_ref),
                (shift_hbm, shift_ref),
            )
        )
    ]
    for load in loads:
        load.start()
    for h in range(H):
        cut = columns(a, h)
        pltpu.make_async_copy(k_ref.at[:, cut], kv.at[key_at(h), b, 0], ksem).start()
        pltpu.make_async_copy(q_ref.at[:, cut], qbuf.at[h, a], zq.at[h]).start()

    loads[0].wait()
    loads[1].wait()
    upper = lax.broadcasted_iota(jnp.int32, (4 * LAT, 2 * hd), 1) < hd
    for quarter in range(A):
        for p in range(PAIRS):
            wide = min(2, H - 2 * p) * hd
            at = (quarter * H + 2 * p) * hd
            w = head_ref[:, at : at + wide]
            if wide > hd:
                zero = jnp.zeros_like(w)
                w = jnp.concatenate(
                    [jnp.where(upper, w, zero), jnp.where(upper, zero, w)], axis=0
                )
            else:
                w = jnp.concatenate([w, jnp.zeros_like(w)], axis=0)
            vsend[quarter, p] = dot_t(v_ref[:, at : at + wide], w).astype(jnp.bfloat16)
    for p in range(PAIRS):
        kv[value_at(p), b, 0] = vsend[a, p]

    for h in range(H):
        drain(kv.at[key_at(h), b, 0], ksem)

    pl.semaphore_wait(barrier, len(partners))

    def scatter(j):
        for d in range(1, A):
            to = lax.rem(a + d, A)
            peer = to * B + b
            if j >= ITEMS:
                h = j - ITEMS
                src = q_ref.at[:, columns(to, h)]
                remote(src, qbuf.at[h, a], zsend.at[1], zq.at[h], peer).start()
            else:
                if j % 3 == 1:
                    src = vsend.at[to, j // 3]
                else:
                    src = k_ref.at[:, columns(to, j - (j + 1) // 3)]
                remote(src, kv.at[j, b, A - d], zsend.at[0], zkv.at[j], peer).start()

    for j in range(WINDOW):
        scatter(j)

    own = kv.at[:, b, 0]
    for d in range(1, BH):
        to = a * B + lax.rem(bh + d, BH) * 2 + core
        remote(own, own, ysend, yown.at[d], to).start()
    remote(own, own, csend, cown.at[0], sibling).start()

    hbuf[...] = jnp.zeros_like(hbuf)
    weights = pltpu.make_async_copy(wm_hbm, wm, wsem)
    weights.start()

    w4[...] = jnp.zeros_like(w4)
    loads[2].wait()
    for ta in range(3):
        for ri in range(2):
            for pc in range(2):
                for tb in range(3):
                    at = (2, 0, 1, 3)[ri + tb] * 4 * LAT + LAT * pc
                    to = (2 * ri + pc) * ch
                    w4[ta, at : at + 3 * LAT, to : to + ch] = wi_ref[3 * ta + tb]
    span = ch // GROUPS

    def group_of(axis):
        at = lax.broadcasted_iota(jnp.int32, (ch, ch), axis).astype(jnp.float32)
        return jnp.floor((at + 0.5) * (1.0 / span))

    gmat[...] = jnp.where(group_of(0) == group_of(1), 1.0, 0.0).astype(jnp.bfloat16)
    def spot_of(shape, lanes):
        src = lax.broadcasted_iota(jnp.int32, shape, 0)
        dst = lax.broadcasted_iota(jnp.int32, shape, 1) % lanes
        return src, dst, (dst // LAT + 1) % 2 * LAT + dst % LAT

    lane_side = lax.broadcasted_iota(jnp.int32, (8 * LAT, 16 * LAT), 1) // (8 * LAT)
    src, dst, inner = spot_of((8 * LAT, 16 * LAT), 8 * LAT)
    wanted = lane_side * 4 * LAT + dst // (4 * LAT) * 2 * LAT + inner
    pick_own[...] = jnp.where(src == wanted, 1.0, 0.0).astype(jnp.bfloat16)
    block = lax.broadcasted_iota(jnp.int32, (16 * LAT, 24 * LAT), 1) // (8 * LAT)
    src, dst, inner = spot_of((16 * LAT, 24 * LAT), 8 * LAT)
    below = dst // (4 * LAT)
    first_at = jnp.where(below == 0, jnp.where(block == 2, 0, 1 + 2 * block), 0)
    last_at = jnp.where(below == 1, jnp.where(block == 2, 1, 2 * block), 0)
    wanted = below * 8 * LAT + (first_at + last_at) * 2 * LAT + inner
    pick_near[...] = jnp.where(src == wanted, 1.0, 0.0).astype(jnp.bfloat16)
    sums[...] = jnp.zeros_like(sums)
    ubuf[...] = jnp.zeros_like(ubuf)
    dbuf[...] = jnp.zeros_like(dbuf)
    loads[3].wait()
    streamed = dot_t(stream_ref[...], head_ref[...])
    streamed = jnp.concatenate([streamed, jnp.zeros_like(streamed)], axis=1)
    sums[pl.ds(pl.multiple_of(a * tok, 8), tok)] = streamed

    def spread_on(j):
        for d in range(1, BH):
            theirs = lax.rem(bh + BH - d, BH) * 2 + core
            slab = kv.at[j, theirs, 1:A]
            drain(slab, yrecv.at[j, d])
            remote(slab, slab, csend, crecv.at[j, d], sibling).start()

    for j in range(ITEMS):
        slab = kv.at[j, b, 1:A]
        drain(slab, zkv.at[j])
        if j + WINDOW < ITEMS + H:
            scatter(j + WINDOW)
        for d in range(1, BH):
            to = a * B + lax.rem(bh + d, BH) * 2 + core
            remote(slab, slab, ysend, yrecv.at[j, d], to).start()
        remote(slab, slab, csend, crecv.at[j, 0], sibling).start()
        if j == LAG - 1:
            for d in range(1, BH):
                theirs = lax.rem(bh + BH - d, BH) * 2 + core
                slab = kv.at[:, theirs, 0]
                drain(slab, yown.at[d])
                remote(slab, slab, csend, cown.at[d], sibling).start()
        if j >= LAG:
            spread_on(j - LAG)
    for j in range(ITEMS + WINDOW, ITEMS + H):
        scatter(j)

    def gathered(j):
        for d in range(BH):
            theirs = lax.rem(bh + BH - d, BH) * 2 + 1 - core
            drain(kv.at[j, theirs, 1:A], crecv.at[j, d])

    side = lax.broadcasted_iota(jnp.int32, (A * tok, 8 * LAT), 1) // (4 * LAT)

    late = ITEMS - LAG
    for h in range(H):
        while late <= BEFORE[h]:
            spread_on(late)
            late += 1
        if h == 0:
            for d in range(BH):
                theirs = lax.rem(bh + BH - d, BH) * 2 + 1 - core
                drain(kv.at[:, theirs, 0], cown.at[d])
        gathered(key_at(h))
        if h % 2 == 0 and h < H - 1:
            gathered(value_at(h // 2))
        drain(qbuf.at[h], zq.at[h])
        query = qbuf[h].reshape(A * tok, hd)
        key = kv[key_at(h)].reshape(n * tok, hd)
        scores = dot_t(query, key)
        top = jnp.max(scores, axis=-1, keepdims=True)
        expo = jnp.exp2((scores - top) * scale)
        total = jnp.sum(expo, axis=-1, keepdims=True)
        weight = expo.astype(jnp.bfloat16)
        if h == H - 1:
            held[...] = weight
            while late < ITEMS:
                spread_on(late)
                late += 1
            gathered(value_at(h // 2))
            weight = held[...]
        value = kv[value_at(h // 2)].reshape(n * tok, 8 * LAT)
        out = dot(weight, value) / total
        sums[...] += jnp.where(side == h % 2, out, 0.0)

    whole = sums[...]
    whole = whole + pltpu.roll(whole, 4 * LAT, 1)
    turned = pltpu.roll(whole, 2 * LAT, 1)
    whole = whole.reshape(A, tok, 8 * LAT)
    turned = turned.reshape(A, tok, 8 * LAT)
    left = lax.broadcasted_iota(jnp.int32, (A, 2 * cols, 8 * LAT), 2) < 4 * LAT
    part[...] = jnp.where(left, whole[:, : 2 * cols], whole[:, cols:]).astype(jnp.bfloat16)
    for d in far_first:
        to = lax.rem(a + d, A)
        remote(part.at[to], lbuf.at[a], lsend, lrecv, to * B + b).start()
    quarter_of = lax.broadcasted_iota(jnp.int32, (A, cols, 8 * LAT), 2) // (2 * LAT)
    thirds = [whole[:, i * cols : (i + 1) * cols] for i in range(2)] + [turned[:, 2 * cols :]]
    upper = jnp.where(quarter_of == 1, thirds[0], jnp.where(quarter_of == 3, thirds[1], thirds[2]))
    lower = jnp.where(quarter_of == 0, thirds[0], jnp.where(quarter_of == 2, thirds[1], thirds[2]))
    upart[...] = upper.astype(jnp.bfloat16)
    dpart[...] = lower.astype(jnp.bfloat16)

    def near_rows(act_on):
        for d in far_first + [0]:
            z = lax.rem(a + d, A)
            row = z * B + b

            @pl.when(row < n - 1)
            def _():
                act_on(remote(upart.at[z], ubuf.at[a], usend, urecv, row + 1))

            @pl.when(row > 0)
            def _():
                act_on(remote(dpart.at[z], dbuf.at[a], dsend, drecv, row - 1))

    near_rows(lambda copy: copy.start())
    lbuf[a] = part[a]
    drain(lbuf.at[0 : A - 1], lrecv)

    @pl.when(me > 0)
    def _():
        drain(ubuf, urecv)

    @pl.when(me < n - 1)
    def _():
        drain(dbuf, drecv)

    def total_of(ref):
        total = ref[0].astype(jnp.float32)
        for d in range(1, A):
            total = total + ref[d].astype(jnp.float32)
        return total.astype(jnp.bfloat16)

    laid = dot(total_of(lbuf), pick_own[...])
    own_rows = jnp.concatenate([laid[:, : 8 * LAT], laid[cols:, 8 * LAT :]], axis=0)
    laid = dot(jnp.concatenate([total_of(ubuf), total_of(dbuf)], axis=1), pick_near[...])
    near_lines = jnp.concatenate(
        [laid[:, i * 8 * LAT : (i + 1) * 8 * LAT] for i in range(3)], axis=0
    )
    laid = jnp.concatenate([own_rows, near_lines], axis=0)
    wide = 8 * LAT
    spot = lax.broadcasted_iota(jnp.int32, (2 * tok, wide), 0) % cols
    piece = lax.broadcasted_iota(jnp.int32, (2 * tok, wide), 1) // LAT % 4
    before = jnp.where(spot == 0, 0.0, pltpu.roll(laid, 1, 0))
    after = jnp.where(spot == cols - 1, 0.0, pltpu.roll(laid, 2 * tok - 1, 0))
    laid = jnp.where(piece == 0, before, jnp.where(piece == 3, after, laid)).astype(jnp.bfloat16)
    near = jnp.concatenate([laid[:tok], laid[tok:]], axis=1)
    first[...] = dot(near, w4[2])
    for ta in (1, 0):
        first[(2 - ta) * cols :] += dot(near[: (ta + 1) * cols], w4[ta])

    edge[...] = first[...].astype(jnp.bfloat16)

    def conv(row, phase):
        if row in (1, 2):
            at = ((row - 1) * 2 + phase) * ch
            return first[:, at : at + ch]
        return hbuf[row // 3, :, phase * ch : (phase + 1) * ch].astype(jnp.float32)

    cells = 4 * tok

    def folded(parts):
        whole = parts[0] + parts[1] + parts[2] + parts[3]
        return jnp.sum(whole, axis=0, keepdims=True)

    own = [conv(1 + ri, pc) for ri in range(2) for pc in range(2)]
    mean = folded(own) / cells
    square = folded([(x - mean) * (x - mean) for x in own])
    pieces = ch // 128
    rows = [x[:, 128 * i : 128 * (i + 1)] for x in (mean, square) for i in range(pieces)]
    sbuf[me, : 2 * pieces] = jnp.concatenate(rows, axis=0)

    @pl.loop(1, n)
    def _(d):
        mine = sbuf.at[me, 0 : 2 * pieces]
        remote(mine, mine, ssend, srecv, lax.rem(me + d, n)).start()

    @pl.when(me > 0)
    def _():
        remote(edge.at[:, : 2 * ch], hbuf.at[1], hsend.at[0], hrecv.at[1], me - 1).start()

    @pl.when(me < n - 1)
    def _():
        remote(edge.at[:, 2 * ch :], hbuf.at[0], hsend.at[1], hrecv.at[0], me + 1).start()

    drain(sbuf.at[0 : n - 1, 0 : 2 * pieces], srecv)

    def grouped(x):
        high = x.astype(jnp.bfloat16).astype(jnp.float32)
        rest = x - high
        middle = rest.astype(jnp.bfloat16).astype(jnp.float32)
        pieces = [high, middle, rest - middle, jnp.zeros((13, ch), jnp.float32)]
        split = jnp.concatenate(pieces, axis=0).astype(jnp.bfloat16)
        return jnp.sum(dot(split, gmat[...]), axis=0, keepdims=True)

    means = jnp.concatenate([sbuf[:, i] for i in range(pieces)], axis=1)
    squares = jnp.concatenate([sbuf[:, pieces + i] for i in range(pieces)], axis=1)
    middle = grouped(jnp.sum(means, axis=0, keepdims=True)) / (n * span)
    apart = means - middle
    spread = jnp.sum(squares + cells * (apart * apart), axis=0, keepdims=True)
    variance = grouped(spread) / (n * span * cells)
    root = jnp.sqrt(variance + 1e-06)

    spot = lax.broadcasted_iota(jnp.int32, (tok, ch), 0) % cols

    def place(row, x0, x1):
        left = jnp.where(spot == 0, 0.0, pltpu.roll(x1, 1, 0))
        right = jnp.where(spot == cols - 1, 0.0, pltpu.roll(x0, tok - 1, 0))
        act[:, row, :, 0:ch] = left.astype(jnp.bfloat16).reshape(frames, cols, ch)
        act[:, row, :, 3 * ch :] = right.astype(jnp.bfloat16).reshape(frames, cols, ch)

    loads[4].wait()
    loads[5].wait()
    gain = gain_ref[...].reshape(1, ch)
    shift = shift_ref[...].reshape(1, ch)

    gain = gain / root

    def active(row, phase):
        y = (conv(row, phase) - middle) * gain + shift
        y = y * jax.nn.sigmoid(y)
        if row == 0:
            y = jnp.where(me > 0, y, 0.0)
        if row == 3:
            y = jnp.where(me < n - 1, y, 0.0)
        return y

    def prepare(row):
        x0 = active(row, 0)
        x1 = active(row, 1)
        act[:, row, :, ch : 2 * ch] = x0.astype(jnp.bfloat16).reshape(frames, cols, ch)
        act[:, row, :, 2 * ch : 3 * ch] = x1.astype(jnp.bfloat16).reshape(frames, cols, ch)
        place(row, x0, x1)

    def tap(ta, tb):
        rows = []
        for f in range(ta + 1):
            for pc in range(2):
                rows.append(
                    act[f, tb : tb + 2, :, pc * ch : (pc + 3) * ch].reshape(2 * cols, 3 * ch)
                )
        return dot(jnp.concatenate(rows, axis=0), wm[3 * ta + tb])

    def taps(tb):
        for ta in (2, 1, 0):
            if tb == 1 and ta == 2:
                acc[...] = tap(ta, tb)
            else:
                acc[(2 - ta) * 4 * cols :] += tap(ta, tb)

    prepare(1)
    prepare(2)
    weights.wait()
    taps(1)

    @pl.when(me > 0)
    def _():
        drain(hbuf.at[0], hrecv.at[0])

    @pl.when(me < n - 1)
    def _():
        drain(hbuf.at[1], hrecv.at[1])

    prepare(0)
    prepare(3)
    taps(0)
    taps(2)

    for f in range(frames):
        for pc in range(2):
            for ri in range(2):
                at = ((f * 2 + pc) * 2 + ri) * cols
                base = own[2 * ri + pc][f * cols : (f + 1) * cols]
                total = base + acc[at : at + cols]
                lines = pl.ds((f * 2 + ri) * 2 * cols + pc, cols, stride=2)
                for i in range(pieces):
                    woven[i, lines] = total[:, 128 * i : 128 * (i + 1)]
    for i in range(pieces):
        out_ref[:, :, :, 128 * i : 128 * (i + 1)] = (
            woven[i].reshape(frames, 2, 2 * cols, 128).astype(jnp.bfloat16)
        )

    drain(kv.at[:, 0, 0 : A - 1], zsend.at[0])
    drain(qbuf.at[:, 0 : A - 1], zsend.at[1])
    if BH > 1:
        drain(kv.at[:, 0 : BH - 1], ysend)
    drain(kv.at[:, 0:BH], csend)
    drain(part.at[0 : A - 1], lsend)
    drain(sbuf.at[0 : n - 1, 0 : 2 * pieces], ssend)

    near_rows(lambda copy: copy.wait_send())

    @pl.when(me > 0)
    def _():
        drain(hbuf.at[0], hsend.at[0])

    @pl.when(me < n - 1)
    def _():
        drain(hbuf.at[1], hsend.at[1])


def shards(
    n,
    queries,
    keys,
    values,
    stream,
    head_weight,
    conv_in_weight,
    norm_gain,
    norm_shift,
    conv_mid_weight,
):
    frames, rows_here, cols, width = queries.shape
    assert frames == 3 and rows_here == 1
    tok = frames * cols
    hd = width // HEADS
    ch = norm_gain.shape[0]
    A = QUARTERS
    B = n // A
    BH = B // 2
    H = HEADS // A
    PAIRS = (H + 1) // 2
    ITEMS = H + PAIRS
    bf16, f32 = jnp.bfloat16, jnp.float32
    vmem = pl.BlockSpec(memory_space=pltpu.VMEM)
    hbm = pl.BlockSpec(memory_space=pl.ANY)
    dma = pltpu.SemaphoreType.DMA
    operands = [
        pltpu.with_memory_space_constraint(x, pltpu.HBM)
        for x in (
            queries.reshape(tok, width),
            keys.reshape(tok, width),
            values.reshape(tok, width),
            stream.reshape(tok, width),
            head_weight.T,
            conv_in_weight.reshape(9, 3 * LAT, ch),
            norm_gain,
            norm_shift,
            conv_mid_weight.reshape(9, 3 * ch, ch),
        )
    ]
    out = pl.pallas_call(
        functools.partial(body, n, frames, cols),
        out_shape=jax.ShapeDtypeStruct((frames, 2, 2 * cols, ch), bf16),
        in_specs=[hbm] * 9,
        out_specs=vmem,
        scratch_shapes=[
            pltpu.VMEM((tok, width), bf16),
            pltpu.VMEM((ch,), f32),
            pltpu.VMEM((ch,), f32),
            pltpu.VMEM((tok, width), bf16),
            pltpu.VMEM((4 * LAT, width), bf16),
            pltpu.VMEM((9, 3 * LAT, ch), bf16),
            pltpu.VMEM((A, PAIRS, tok, 8 * LAT), bf16),
            pltpu.VMEM((H, A, tok, hd), bf16),
            pltpu.VMEM((ITEMS, B, A, tok, hd), bf16),
            pltpu.VMEM((A * tok, 8 * LAT), f32),
            pltpu.VMEM((A, 2 * cols, 8 * LAT), bf16),
            pltpu.VMEM((A, 2 * cols, 8 * LAT), bf16),
            pltpu.VMEM((A, cols, 8 * LAT), bf16),
            pltpu.VMEM((A, cols, 8 * LAT), bf16),
            pltpu.VMEM((A, cols, 8 * LAT), bf16),
            pltpu.VMEM((A, cols, 8 * LAT), bf16),
            pltpu.VMEM((8 * LAT, 16 * LAT), bf16),
            pltpu.VMEM((16 * LAT, 24 * LAT), bf16),
            pltpu.VMEM((tok, 4 * ch), bf16),
            pltpu.VMEM((2, tok, 2 * ch), bf16),
            pltpu.VMEM((A * tok, n * tok), bf16),
            pltpu.VMEM((3, 16 * LAT, 4 * ch), bf16),
            pltpu.VMEM((9, 3 * ch, ch), bf16),
            pltpu.VMEM((ch, ch), bf16),
            pltpu.VMEM((tok, 4 * ch), f32),
            pltpu.VMEM((frames, 4, cols, 4 * ch), bf16),
            pltpu.VMEM((4 * tok, ch), f32),
            pltpu.VMEM((ch // 128, 4 * tok, 128), f32),
            pltpu.VMEM((n, 8, 128), f32),
            dma((2,)),
            dma((H,)),
            dma((ITEMS,)),
            dma,
            dma,
            dma((ITEMS, BH)),
            dma((BH,)),
            dma((BH,)),
            dma,
            dma,
            dma((ITEMS, BH)),
            dma,
            dma,
            dma,
            dma,
            dma,
            dma,
            dma((2,)),
            dma((2,)),
            dma,
            dma,
            dma,
            dma((6,)),
        ],
        compiler_params=pltpu.CompilerParams(
            collective_id=0, has_side_effects=True, vmem_limit_bytes=44 * 2**20
        ),
        name="decode",
    )(*operands)
    return out


def solution(mesh):
    row = P("groups", "seq", None, None)
    return jax.shard_map(
        functools.partial(shards, mesh.shape["seq"]),
        mesh=mesh,
        in_specs=(row, row, row, row, P(), P(), P(), P(), P()),
        out_specs=row,
        check_vma=False,
    )
```

```python
import functools
import math

import jax
import jax.numpy as jnp
from jax import lax
from jax.experimental import pallas as pl
from jax.experimental.pallas import tpu as pltpu
from jax.sharding import PartitionSpec as P

HEADS = 20
GROUPS = 32
QUARTERS = 4
BEFORE = (4, 5, 6, 7, 7)
LAG = 4
WINDOW = 7
LAT = 16
NT = (((1,), (1,)), ((), ()))


def dot(a, b):
    return jnp.dot(a, b, preferred_element_type=jnp.float32)


def dot_t(a, b):
    return lax.dot_general(a, b, NT, preferred_element_type=jnp.float32)


def body(
    n,
    frames,
    cols,
    q_ref,
    k_ref,
    v_hbm,
    stream_hbm,
    head_hbm,
    wi_hbm,
    gain_hbm,
    shift_hbm,
    wm_hbm,
    out_ref,
    v_ref,
    gain_ref,
    shift_ref,
    stream_ref,
    head_ref,
    wi_ref,
    vsend,
    qbuf,
    kv,
    sums,
    part,
    lbuf,
    upart,
    ubuf,
    dpart,
    dbuf,
    pick_own,
    pick_near,
    edge,
    hbuf,
    held,
    w4,
    wm,
    gmat,
    first,
    act,
    acc,
    woven,
    sbuf,
    zsend,
    zq,
    zkv,
    loc,
    ysend,
    yrecv,
    yown,
    cown,
    ksem,
    csend,
    crecv,
    lsend,
    lrecv,
    usend,
    urecv,
    dsend,
    drecv,
    hsend,
    hrecv,
    ssend,
    srecv,
    wsem,
    isem,
):
    A = QUARTERS
    B = n // A
    BH = B // 2
    H = HEADS // A
    PAIRS = (H + 1) // 2
    ITEMS = H + PAIRS
    tok = frames * cols
    hd = q_ref.shape[1] // HEADS
    ch = gain_ref.shape[0]
    scale = math.log2(math.e) / hd**0.5
    me = lax.axis_index("seq")
    a = me // B
    b = me % B
    bh = b // 2
    core = b % 2
    sibling = me + 1 - 2 * core

    def remote(src, dst, ssem, rsem, to):
        return pltpu.make_async_remote_copy(
            src_ref=src,
            dst_ref=dst,
            send_sem=ssem,
            recv_sem=rsem,
            device_id={"seq": to},
            device_id_type=pl.DeviceIdType.MESH,
        )

    def drain(ref, sem):
        pltpu.make_async_copy(ref, ref, sem).wait()

    def columns(quarter, h):
        return pl.ds(pl.multiple_of((quarter * H + h) * hd, hd), hd)

    def key_at(h):
        return h + (h + 1) // 2

    def rows_of_item(j):
        return slice(0, 2 * cols if j == ITEMS - 1 else tok)

    def value_at(p):
        return 3 * p + 1

    low = (A - 1 - a) // (A - 1)
    high = a // (A - 1)
    far_first = [2 + low - high, 3 - high - low, 1 + 2 * high]
    barrier = pltpu.get_barrier_semaphore()
    partners = [lax.rem(a + d, A) * B + b for d in range(1, A)]
    partners += [a * B + lax.rem(bh + d, BH) * 2 + core for d in range(1, BH)]
    partners.append(sibling)
    for to in partners:
        pl.semaphore_signal(
            barrier, inc=1, device_id={"seq": to}, device_id_type=pl.DeviceIdType.MESH
        )

    loads = [
        pltpu.make_async_copy(src, dst, isem.at[i])
        for i, (src, dst) in enumerate(
            (
                (v_hbm, v_ref),
                (head_hbm, head_ref),
                (wi_hbm, wi_ref),
                (stream_hbm, stream_ref),
                (gain_hbm, gain_ref),
                (shift_hbm, shift_ref),
            )
        )
    ]
    for load in loads:
        load.start()
    for h in range(H):
        cut = columns(a, h)
        pltpu.make_async_copy(k_ref.at[:, cut], kv.at[key_at(h), b, 0], ksem).start()
        pltpu.make_async_copy(q_ref.at[:, cut], qbuf.at[h, a], zq.at[h]).start()

    loads[0].wait()
    loads[1].wait()
    upper = lax.broadcasted_iota(jnp.int32, (4 * LAT, 2 * hd), 1) < hd
    for quarter in range(A):
        for p in range(PAIRS):
            wide = min(2, H - 2 * p) * hd
            at = (quarter * H + 2 * p) * hd
            w = head_ref[:, at : at + wide]
            if wide > hd:
                zero = jnp.zeros_like(w)
                w = jnp.concatenate(
                    [jnp.where(upper, w, zero), jnp.where(upper, zero, w)], axis=0
                )
            else:
                w = jnp.concatenate([w, w], axis=0)
            projected = dot_t(v_ref[:, at : at + wide], w).astype(jnp.bfloat16)
            if wide == hd:
                blank = jnp.zeros((cols, 8 * LAT), jnp.bfloat16)
                moved = jnp.concatenate([projected[2 * cols :], blank], axis=0)
                here = lax.broadcasted_iota(jnp.int32, (2 * cols, 8 * LAT), 1) < 4 * LAT
                projected = jnp.concatenate(
                    [jnp.where(here, projected[: 2 * cols], moved), blank], axis=0
                )
            vsend[quarter, p] = projected
    for p in range(PAIRS):
        kv[value_at(p), b, 0] = vsend[a, p]

    for h in range(H):
        drain(kv.at[key_at(h), b, 0], ksem)

    pl.semaphore_wait(barrier, len(partners))

    def scatter(j):
        for d in range(1, A):
            to = lax.rem(a + d, A)
            peer = to * B + b
            if j >= ITEMS:
                h = j - ITEMS
                src = q_ref.at[:, columns(to, h)]
                remote(src, qbuf.at[h, a], zsend.at[1], zq.at[h], peer).start()
            else:
                if j % 3 == 1:
                    src = vsend.at[to, j // 3, rows_of_item(j)]
                else:
                    src = k_ref.at[:, columns(to, j - (j + 1) // 3)]
                remote(
                    src, kv.at[j, b, A - d, rows_of_item(j)], zsend.at[0], zkv.at[j], peer
                ).start()

    for j in range(WINDOW):
        scatter(j)

    own = kv.at[:, b, 0]
    for d in range(1, BH):
        to = a * B + lax.rem(bh + d, BH) * 2 + core
        remote(own, own, ysend, yown.at[d], to).start()
    remote(own, own, csend, cown.at[0], sibling).start()

    hbuf[...] = jnp.zeros_like(hbuf)
    weights = pltpu.make_async_copy(wm_hbm, wm, wsem)
    weights.start()

    w4[...] = jnp.zeros_like(w4)
    loads[2].wait()
    for ta in range(3):
        for ri in range(2):
            for pc in range(2):
                for tb in range(3):
                    at = (2, 0, 1, 3)[ri + tb] * 4 * LAT + LAT * pc
                    to = (2 * ri + pc) * ch
                    w4[ta, at : at + 3 * LAT, to : to + ch] = wi_ref[3 * ta + tb]
    span = ch // GROUPS

    def group_of(axis):
        at = lax.broadcasted_iota(jnp.int32, (ch, ch), axis).astype(jnp.float32)
        return jnp.floor((at + 0.5) * (1.0 / span))

    gmat[...] = jnp.where(group_of(0) == group_of(1), 1.0, 0.0).astype(jnp.bfloat16)
    def spot_of(shape, lanes):
        src = lax.broadcasted_iota(jnp.int32, shape, 0)
        dst = lax.broadcasted_iota(jnp.int32, shape, 1) % lanes
        return src, dst, (dst // LAT + 1) % 2 * LAT + dst % LAT

    lane_side = lax.broadcasted_iota(jnp.int32, (8 * LAT, 16 * LAT), 1) // (8 * LAT)
    src, dst, inner = spot_of((8 * LAT, 16 * LAT), 8 * LAT)
    wanted = lane_side * 4 * LAT + dst // (4 * LAT) * 2 * LAT + inner
    pick_own[...] = jnp.where(src == wanted, 1.0, 0.0).astype(jnp.bfloat16)
    block = lax.broadcasted_iota(jnp.int32, (16 * LAT, 24 * LAT), 1) // (8 * LAT)
    src, dst, inner = spot_of((16 * LAT, 24 * LAT), 8 * LAT)
    below = dst // (4 * LAT)
    first_at = jnp.where(below == 0, jnp.where(block == 2, 0, 1 + 2 * block), 0)
    last_at = jnp.where(below == 1, jnp.where(block == 2, 1, 2 * block), 0)
    wanted = below * 8 * LAT + (first_at + last_at) * 2 * LAT + inner
    pick_near[...] = jnp.where(src == wanted, 1.0, 0.0).astype(jnp.bfloat16)
    sums[...] = jnp.zeros_like(sums)
    ubuf[...] = jnp.zeros_like(ubuf)
    dbuf[...] = jnp.zeros_like(dbuf)
    loads[3].wait()
    streamed = dot_t(stream_ref[...], head_ref[...])
    streamed = jnp.concatenate([streamed, jnp.zeros_like(streamed)], axis=1)
    sums[pl.ds(pl.multiple_of(a * tok, 8), tok)] = streamed

    def spread_on(j):
        for d in range(1, BH):
            theirs = lax.rem(bh + BH - d, BH) * 2 + core
            slab = kv.at[j, theirs, 1:A, rows_of_item(j)]
            drain(slab, yrecv.at[j, d])
            remote(slab, slab, csend, crecv.at[j, d], sibling).start()

    for j in range(ITEMS):
        slab = kv.at[j, b, 1:A, rows_of_item(j)]
        drain(slab, zkv.at[j])
        if j + WINDOW < ITEMS + H:
            scatter(j + WINDOW)
        for d in range(1, BH):
            to = a * B + lax.rem(bh + d, BH) * 2 + core
            remote(slab, slab, ysend, yrecv.at[j, d], to).start()
        remote(slab, slab, csend, crecv.at[j, 0], sibling).start()
        if j == LAG - 1:
            for d in range(1, BH):
                theirs = lax.rem(bh + BH - d, BH) * 2 + core
                slab = kv.at[:, theirs, 0]
                drain(slab, yown.at[d])
                remote(slab, slab, csend, cown.at[d], sibling).start()
        if j >= LAG:
            spread_on(j - LAG)
    for j in range(ITEMS + WINDOW, ITEMS + H):
        scatter(j)

    def gathered(j):
        for d in range(BH):
            theirs = lax.rem(bh + BH - d, BH) * 2 + 1 - core
            drain(kv.at[j, theirs, 1:A, rows_of_item(j)], crecv.at[j, d])

    side = lax.broadcasted_iota(jnp.int32, (A * tok, 8 * LAT), 1) // (4 * LAT)

    late = ITEMS - LAG
    for h in range(H):
        while late <= BEFORE[h]:
            spread_on(late)
            late += 1
        if h == 0:
            for d in range(BH):
                theirs = lax.rem(bh + BH - d, BH) * 2 + 1 - core
                drain(kv.at[:, theirs, 0], cown.at[d])
        gathered(key_at(h))
        if h % 2 == 0 and h < H - 1:
            gathered(value_at(h // 2))
        drain(qbuf.at[h], zq.at[h])
        query = qbuf[h].reshape(A * tok, hd)
        if h == H - 1:
            key = jnp.concatenate(
                [
                    kv[key_at(h), :, :, : 2 * cols].reshape(2 * n * cols, hd),
                    kv[key_at(h), :, :, 2 * cols :].reshape(n * cols, hd),
                ],
                axis=0,
            )
        else:
            key = kv[key_at(h)].reshape(n * tok, hd)
        scores = dot_t(query, key)
        top = jnp.max(scores, axis=-1, keepdims=True)
        expo = jnp.exp2((scores - top) * scale)
        total = jnp.sum(expo, axis=-1, keepdims=True)
        weight = expo.astype(jnp.bfloat16)
        if h == H - 1:
            held[...] = weight
            while late < ITEMS:
                spread_on(late)
                late += 1
            gathered(value_at(h // 2))
            value = kv[value_at(h // 2), :, :, : 2 * cols]
            out = jnp.where(
                side == 0,
                dot(held[:, : 2 * n * cols], value.reshape(2 * n * cols, 8 * LAT)),
                dot(held[:, 2 * n * cols :], value[:, :, :cols].reshape(n * cols, 8 * LAT)),
            )
            sums[...] += out / total
        else:
            value = kv[value_at(h // 2)].reshape(n * tok, 8 * LAT)
            out = dot(weight, value) / total
            sums[...] += jnp.where(side == h % 2, out, 0.0)

    whole = sums[...]
    whole = whole + pltpu.roll(whole, 4 * LAT, 1)
    turned = pltpu.roll(whole, 2 * LAT, 1)
    whole = whole.reshape(A, tok, 8 * LAT)
    turned = turned.reshape(A, tok, 8 * LAT)
    left = lax.broadcasted_iota(jnp.int32, (A, 2 * cols, 8 * LAT), 2) < 4 * LAT
    part[...] = jnp.where(left, whole[:, : 2 * cols], whole[:, cols:]).astype(jnp.bfloat16)
    for d in far_first:
        to = lax.rem(a + d, A)
        remote(part.at[to], lbuf.at[a], lsend, lrecv, to * B + b).start()
    quarter_of = lax.broadcasted_iota(jnp.int32, (A, cols, 8 * LAT), 2) // (2 * LAT)
    thirds = [whole[:, i * cols : (i + 1) * cols] for i in range(2)] + [turned[:, 2 * cols :]]
    upper = jnp.where(quarter_of == 1, thirds[0], jnp.where(quarter_of == 3, thirds[1], thirds[2]))
    lower = jnp.where(quarter_of == 0, thirds[0], jnp.where(quarter_of == 2, thirds[1], thirds[2]))
    upart[...] = upper.astype(jnp.bfloat16)
    dpart[...] = lower.astype(jnp.bfloat16)

    def near_rows(act_on):
        for d in far_first + [0]:
            z = lax.rem(a + d, A)
            row = z * B + b

            @pl.when(row < n - 1)
            def _():
                act_on(remote(upart.at[z], ubuf.at[a], usend, urecv, row + 1))

            @pl.when(row > 0)
            def _():
                act_on(remote(dpart.at[z], dbuf.at[a], dsend, drecv, row - 1))

    near_rows(lambda copy: copy.start())
    lbuf[a] = part[a]
    drain(lbuf.at[0 : A - 1], lrecv)

    @pl.when(me > 0)
    def _():
        drain(ubuf, urecv)

    @pl.when(me < n - 1)
    def _():
        drain(dbuf, drecv)

    def total_of(ref):
        total = ref[0].astype(jnp.float32)
        for d in range(1, A):
            total = total + ref[d].astype(jnp.float32)
        return total.astype(jnp.bfloat16)

    laid = dot(total_of(lbuf), pick_own[...])
    own_rows = jnp.concatenate([laid[:, : 8 * LAT], laid[cols:, 8 * LAT :]], axis=0)
    laid = dot(jnp.concatenate([total_of(ubuf), total_of(dbuf)], axis=1), pick_near[...])
    near_lines = jnp.concatenate(
        [laid[:, i * 8 * LAT : (i + 1) * 8 * LAT] for i in range(3)], axis=0
    )
    laid = jnp.concatenate([own_rows, near_lines], axis=0)
    wide = 8 * LAT
    spot = lax.broadcasted_iota(jnp.int32, (2 * tok, wide), 0) % cols
    piece = lax.broadcasted_iota(jnp.int32, (2 * tok, wide), 1) // LAT % 4
    before = jnp.where(spot == 0, 0.0, pltpu.roll(laid, 1, 0))
    after = jnp.where(spot == cols - 1, 0.0, pltpu.roll(laid, 2 * tok - 1, 0))
    laid = jnp.where(piece == 0, before, jnp.where(piece == 3, after, laid)).astype(jnp.bfloat16)
    near = jnp.concatenate([laid[:tok], laid[tok:]], axis=1)
    first[...] = dot(near, w4[2])
    for ta in (1, 0):
        first[(2 - ta) * cols :] += dot(near[: (ta + 1) * cols], w4[ta])

    edge[...] = first[...].astype(jnp.bfloat16)

    def conv(row, phase):
        if row in (1, 2):
            at = ((row - 1) * 2 + phase) * ch
            return first[:, at : at + ch]
        return hbuf[row // 3, :, phase * ch : (phase + 1) * ch].astype(jnp.float32)

    cells = 4 * tok

    def folded(parts):
        whole = parts[0] + parts[1] + parts[2] + parts[3]
        return jnp.sum(whole, axis=0, keepdims=True)

    own = [conv(1 + ri, pc) for ri in range(2) for pc in range(2)]
    mean = folded(own) / cells
    square = folded([(x - mean) * (x - mean) for x in own])
    pieces = ch // 128
    rows = [x[:, 128 * i : 128 * (i + 1)] for x in (mean, square) for i in range(pieces)]
    sbuf[me, : 2 * pieces] = jnp.concatenate(rows, axis=0)

    @pl.loop(1, n)
    def _(d):
        mine = sbuf.at[me, 0 : 2 * pieces]
        remote(mine, mine, ssend, srecv, lax.rem(me + d, n)).start()

    @pl.when(me > 0)
    def _():
        remote(edge.at[:, : 2 * ch], hbuf.at[1], hsend.at[0], hrecv.at[1], me - 1).start()

    @pl.when(me < n - 1)
    def _():
        remote(edge.at[:, 2 * ch :], hbuf.at[0], hsend.at[1], hrecv.at[0], me + 1).start()

    drain(sbuf.at[0 : n - 1, 0 : 2 * pieces], srecv)

    def grouped(x):
        high = x.astype(jnp.bfloat16).astype(jnp.float32)
        rest = x - high
        middle = rest.astype(jnp.bfloat16).astype(jnp.float32)
        pieces = [high, middle, rest - middle, jnp.zeros((13, ch), jnp.float32)]
        split = jnp.concatenate(pieces, axis=0).astype(jnp.bfloat16)
        return jnp.sum(dot(split, gmat[...]), axis=0, keepdims=True)

    means = jnp.concatenate([sbuf[:, i] for i in range(pieces)], axis=1)
    squares = jnp.concatenate([sbuf[:, pieces + i] for i in range(pieces)], axis=1)
    middle = grouped(jnp.sum(means, axis=0, keepdims=True)) / (n * span)
    apart = means - middle
    spread = jnp.sum(squares + cells * (apart * apart), axis=0, keepdims=True)
    variance = grouped(spread) / (n * span * cells)
    root = jnp.sqrt(variance + 1e-06)

    spot = lax.broadcasted_iota(jnp.int32, (tok, ch), 0) % cols

    def place(row, x0, x1):
        left = jnp.where(spot == 0, 0.0, pltpu.roll(x1, 1, 0))
        right = jnp.where(spot == cols - 1, 0.0, pltpu.roll(x0, tok - 1, 0))
        act[:, row, :, 0:ch] = left.astype(jnp.bfloat16).reshape(frames, cols, ch)
        act[:, row, :, 3 * ch :] = right.astype(jnp.bfloat16).reshape(frames, cols, ch)

    loads[4].wait()
    loads[5].wait()
    gain = gain_ref[...].reshape(1, ch)
    shift = shift_ref[...].reshape(1, ch)

    gain = gain / root

    def active(row, phase):
        y = (conv(row, phase) - middle) * gain + shift
        y = y * jax.nn.sigmoid(y)
        if row == 0:
            y = jnp.where(me > 0, y, 0.0)
        if row == 3:
            y = jnp.where(me < n - 1, y, 0.0)
        return y

    def prepare(row):
        x0 = active(row, 0)
        x1 = active(row, 1)
        act[:, row, :, ch : 2 * ch] = x0.astype(jnp.bfloat16).reshape(frames, cols, ch)
        act[:, row, :, 2 * ch : 3 * ch] = x1.astype(jnp.bfloat16).reshape(frames, cols, ch)
        place(row, x0, x1)

    def tap(ta, tb):
        rows = []
        for f in range(ta + 1):
            for pc in range(2):
                rows.append(
                    act[f, tb : tb + 2, :, pc * ch : (pc + 3) * ch].reshape(2 * cols, 3 * ch)
                )
        return dot(jnp.concatenate(rows, axis=0), wm[3 * ta + tb])

    def taps(tb):
        for ta in (2, 1, 0):
            if tb == 1 and ta == 2:
                acc[...] = tap(ta, tb)
            else:
                acc[(2 - ta) * 4 * cols :] += tap(ta, tb)

    prepare(1)
    prepare(2)
    weights.wait()
    taps(1)

    @pl.when(me > 0)
    def _():
        drain(hbuf.at[0], hrecv.at[0])

    @pl.when(me < n - 1)
    def _():
        drain(hbuf.at[1], hrecv.at[1])

    prepare(0)
    prepare(3)
    taps(0)
    taps(2)

    for f in range(frames):
        for pc in range(2):
            for ri in range(2):
                at = ((f * 2 + pc) * 2 + ri) * cols
                base = own[2 * ri + pc][f * cols : (f + 1) * cols]
                total = base + acc[at : at + cols]
                lines = pl.ds((f * 2 + ri) * 2 * cols + pc, cols, stride=2)
                for i in range(pieces):
                    woven[i, lines] = total[:, 128 * i : 128 * (i + 1)]
    for i in range(pieces):
        out_ref[:, :, :, 128 * i : 128 * (i + 1)] = (
            woven[i].reshape(frames, 2, 2 * cols, 128).astype(jnp.bfloat16)
        )

    drain(kv.at[0 : ITEMS - 1, 0, 0 : A - 1], zsend.at[0])
    drain(kv.at[ITEMS - 1, 0, 0 : A - 1, rows_of_item(ITEMS - 1)], zsend.at[0])
    drain(qbuf.at[:, 0 : A - 1], zsend.at[1])
    if BH > 1:
        drain(kv.at[0 : ITEMS - 1, 0 : BH - 1], ysend)
        drain(kv.at[ITEMS - 1, 0 : BH - 1, 0], ysend)
        drain(kv.at[ITEMS - 1, 0 : BH - 1, 1:A, rows_of_item(ITEMS - 1)], ysend)
    drain(kv.at[0 : ITEMS - 1, 0:BH], csend)
    drain(kv.at[ITEMS - 1, 0:BH, 0], csend)
    drain(kv.at[ITEMS - 1, 0:BH, 1:A, rows_of_item(ITEMS - 1)], csend)
    drain(part.at[0 : A - 1], lsend)
    drain(sbuf.at[0 : n - 1, 0 : 2 * pieces], ssend)

    near_rows(lambda copy: copy.wait_send())

    @pl.when(me > 0)
    def _():
        drain(hbuf.at[0], hsend.at[0])

    @pl.when(me < n - 1)
    def _():
        drain(hbuf.at[1], hsend.at[1])


def shards(
    n,
    queries,
    keys,
    values,
    stream,
    head_weight,
    conv_in_weight,
    norm_gain,
    norm_shift,
    conv_mid_weight,
):
    frames, rows_here, cols, width = queries.shape
    assert frames == 3 and rows_here == 1
    tok = frames * cols
    hd = width // HEADS
    ch = norm_gain.shape[0]
    A = QUARTERS
    B = n // A
    BH = B // 2
    H = HEADS // A
    PAIRS = (H + 1) // 2
    ITEMS = H + PAIRS
    bf16, f32 = jnp.bfloat16, jnp.float32
    vmem = pl.BlockSpec(memory_space=pltpu.VMEM)
    hbm = pl.BlockSpec(memory_space=pl.ANY)
    dma = pltpu.SemaphoreType.DMA
    operands = [
        pltpu.with_memory_space_constraint(x, pltpu.HBM)
        for x in (
            queries.reshape(tok, width),
            keys.reshape(tok, width),
            values.reshape(tok, width),
            stream.reshape(tok, width),
            head_weight.T,
            conv_in_weight.reshape(9, 3 * LAT, ch),
            norm_gain,
            norm_shift,
            conv_mid_weight.reshape(9, 3 * ch, ch),
        )
    ]
    out = pl.pallas_call(
        functools.partial(body, n, frames, cols),
        out_shape=jax.ShapeDtypeStruct((frames, 2, 2 * cols, ch), bf16),
        in_specs=[hbm] * 9,
        out_specs=vmem,
        scratch_shapes=[
            pltpu.VMEM((tok, width), bf16),
            pltpu.VMEM((ch,), f32),
            pltpu.VMEM((ch,), f32),
            pltpu.VMEM((tok, width), bf16),
            pltpu.VMEM((4 * LAT, width), bf16),
            pltpu.VMEM((9, 3 * LAT, ch), bf16),
            pltpu.VMEM((A, PAIRS, tok, 8 * LAT), bf16),
            pltpu.VMEM((H, A, tok, hd), bf16),
            pltpu.VMEM((ITEMS, B, A, tok, hd), bf16),
            pltpu.VMEM((A * tok, 8 * LAT), f32),
            pltpu.VMEM((A, 2 * cols, 8 * LAT), bf16),
            pltpu.VMEM((A, 2 * cols, 8 * LAT), bf16),
            pltpu.VMEM((A, cols, 8 * LAT), bf16),
            pltpu.VMEM((A, cols, 8 * LAT), bf16),
            pltpu.VMEM((A, cols, 8 * LAT), bf16),
            pltpu.VMEM((A, cols, 8 * LAT), bf16),
            pltpu.VMEM((8 * LAT, 16 * LAT), bf16),
            pltpu.VMEM((16 * LAT, 24 * LAT), bf16),
            pltpu.VMEM((tok, 4 * ch), bf16),
            pltpu.VMEM((2, tok, 2 * ch), bf16),
            pltpu.VMEM((A * tok, n * tok), bf16),
            pltpu.VMEM((3, 16 * LAT, 4 * ch), bf16),
            pltpu.VMEM((9, 3 * ch, ch), bf16),
            pltpu.VMEM((ch, ch), bf16),
            pltpu.VMEM((tok, 4 * ch), f32),
            pltpu.VMEM((frames, 4, cols, 4 * ch), bf16),
            pltpu.VMEM((4 * tok, ch), f32),
            pltpu.VMEM((ch // 128, 4 * tok, 128), f32),
            pltpu.VMEM((n, 8, 128), f32),
            dma((2,)),
            dma((H,)),
            dma((ITEMS,)),
            dma,
            dma,
            dma((ITEMS, BH)),
            dma((BH,)),
            dma((BH,)),
            dma,
            dma,
            dma((ITEMS, BH)),
            dma,
            dma,
            dma,
            dma,
            dma,
            dma,
            dma((2,)),
            dma((2,)),
            dma,
            dma,
            dma,
            dma((6,)),
        ],
        compiler_params=pltpu.CompilerParams(
            collective_id=0, has_side_effects=True, vmem_limit_bytes=44 * 2**20
        ),
        name="decode",
    )(*operands)
    return out


def solution(mesh):
    row = P("groups", "seq", None, None)
    return jax.shard_map(
        functools.partial(shards, mesh.shape["seq"]),
        mesh=mesh,
        in_specs=(row, row, row, row, P(), P(), P(), P(), P()),
        out_specs=row,
        check_vma=False,
    )
```

```python
import functools
import math

import jax
import jax.numpy as jnp
from jax import lax
from jax.experimental import pallas as pl
from jax.experimental.pallas import tpu as pltpu
from jax.sharding import PartitionSpec as P

HEADS = 20
GROUPS = 32
QUARTERS = 4
BEFORE = (4, 5, 6, 7, 7)
LAG = 4
WINDOW = 7
LAT = 16
NT = (((1,), (1,)), ((), ()))


def dot(a, b):
    return jnp.dot(a, b, preferred_element_type=jnp.float32)


def dot_t(a, b):
    return lax.dot_general(a, b, NT, preferred_element_type=jnp.float32)


def body(
    n,
    frames,
    cols,
    q_ref,
    k_ref,
    v_hbm,
    stream_hbm,
    head_hbm,
    wi_hbm,
    gain_hbm,
    shift_hbm,
    wm_hbm,
    out_ref,
    v_ref,
    gain_ref,
    shift_ref,
    stream_ref,
    head_ref,
    wi_ref,
    vsend,
    qbuf,
    kv,
    sums,
    part,
    lbuf,
    upart,
    ubuf,
    dpart,
    dbuf,
    pick_own,
    pick_near,
    edge,
    hbuf,
    held,
    w4,
    wm,
    gmat,
    first,
    act,
    acc,
    woven,
    sbuf,
    zsend,
    zq,
    zkv,
    loc,
    ysend,
    yrecv,
    yown,
    cown,
    ksem,
    csend,
    crecv,
    lsend,
    lrecv,
    usend,
    urecv,
    dsend,
    drecv,
    hsend,
    hrecv,
    ssend,
    srecv,
    wsem,
    isem,
):
    A = QUARTERS
    B = n // A
    BH = B // 2
    H = HEADS // A
    PAIRS = (H + 1) // 2
    ITEMS = H + PAIRS
    tok = frames * cols
    hd = q_ref.shape[1] // HEADS
    ch = gain_ref.shape[0]
    scale = math.log2(math.e) / hd**0.5
    me = lax.axis_index("seq")
    a = me // B
    b = me % B
    bh = b // 2
    core = b % 2
    sibling = me + 1 - 2 * core

    def remote(src, dst, ssem, rsem, to):
        return pltpu.make_async_remote_copy(
            src_ref=src,
            dst_ref=dst,
            send_sem=ssem,
            recv_sem=rsem,
            device_id={"seq": to},
            device_id_type=pl.DeviceIdType.MESH,
        )

    def drain(ref, sem):
        pltpu.make_async_copy(ref, ref, sem).wait()

    def columns(quarter, h):
        return pl.ds(pl.multiple_of((quarter * H + h) * hd, hd), hd)

    def key_at(h):
        return h + (h + 1) // 2

    def rows_of_item(j):
        return slice(0, 2 * cols if j == ITEMS - 1 else tok)

    def value_at(p):
        return 3 * p + 1

    low = (A - 1 - a) // (A - 1)
    high = a // (A - 1)
    far_first = [2 + low - high, 3 - high - low, 1 + 2 * high]
    barrier = pltpu.get_barrier_semaphore()
    partners = [lax.rem(a + d, A) * B + b for d in range(1, A)]
    partners += [a * B + lax.rem(bh + d, BH) * 2 + core for d in range(1, BH)]
    partners.append(sibling)
    for to in partners:
        pl.semaphore_signal(
            barrier, inc=1, device_id={"seq": to}, device_id_type=pl.DeviceIdType.MESH
        )

    loads = [
        pltpu.make_async_copy(src, dst, isem.at[i])
        for i, (src, dst) in enumerate(
            (
                (v_hbm, v_ref),
                (head_hbm, head_ref),
                (wi_hbm, wi_ref),
                (stream_hbm, stream_ref),
                (gain_hbm, gain_ref),
                (shift_hbm, shift_ref),
            )
        )
    ]
    for load in loads:
        load.start()
    for h in range(H):
        cut = columns(a, h)
        pltpu.make_async_copy(k_ref.at[:, cut], kv.at[key_at(h), b, 0], ksem).start()
        pltpu.make_async_copy(q_ref.at[:, cut], qbuf.at[h, a], zq.at[h]).start()

    loads[0].wait()
    loads[1].wait()
    upper = lax.broadcasted_iota(jnp.int32, (4 * LAT, 2 * hd), 1) < hd
    for quarter in range(A):
        for p in range(PAIRS):
            wide = min(2, H - 2 * p) * hd
            at = (quarter * H + 2 * p) * hd
            w = head_ref[:, at : at + wide]
            if wide > hd:
                zero = jnp.zeros_like(w)
                w = jnp.concatenate(
                    [jnp.where(upper, w, zero), jnp.where(upper, zero, w)], axis=0
                )
            else:
                w = jnp.concatenate([w, w], axis=0)
            projected = dot_t(v_ref[:, at : at + wide], w).astype(jnp.bfloat16)
            if wide == hd:
                blank = jnp.zeros((cols, 8 * LAT), jnp.bfloat16)
                moved = jnp.concatenate([projected[2 * cols :], blank], axis=0)
                here = lax.broadcasted_iota(jnp.int32, (2 * cols, 8 * LAT), 1) < 4 * LAT
                projected = jnp.concatenate(
                    [jnp.where(here, projected[: 2 * cols], moved), blank], axis=0
                )
            vsend[quarter, p] = projected
    for p in range(PAIRS):
        kv[value_at(p), b, 0] = vsend[a, p]

    for h in range(H):
        drain(kv.at[key_at(h), b, 0], ksem)

    pl.semaphore_wait(barrier, len(partners))

    def scatter(j):
        for d in range(1, A):
            to = lax.rem(a + d, A)
            peer = to * B + b
            if j >= ITEMS:
                h = j - ITEMS
                src = q_ref.at[:, columns(to, h)]
                remote(src, qbuf.at[h, a], zsend.at[1], zq.at[h], peer).start()
            else:
                if j % 3 == 1:
                    src = vsend.at[to, j // 3, rows_of_item(j)]
                else:
                    src = k_ref.at[:, columns(to, j - (j + 1) // 3)]
                remote(
                    src, kv.at[j, b, A - d, rows_of_item(j)], zsend.at[0], zkv.at[j], peer
                ).start()

    for j in range(WINDOW):
        scatter(j)

    own = kv.at[:, b, 0]
    for d in range(1, BH):
        to = a * B + lax.rem(bh + d, BH) * 2 + core
        remote(own, own, ysend, yown.at[d], to).start()
    remote(own, own, csend, cown.at[0], sibling).start()

    hbuf[...] = jnp.zeros_like(hbuf)
    weights = pltpu.make_async_copy(wm_hbm, wm, wsem)
    weights.start()

    w4[...] = jnp.zeros_like(w4)
    loads[2].wait()
    for ta in range(3):
        for ri in range(2):
            for pc in range(2):
                for tb in range(3):
                    at = (2, 0, 1, 3)[ri + tb] * 4 * LAT + LAT * pc
                    to = (2 * ri + pc) * ch
                    w4[ta, at : at + 3 * LAT, to : to + ch] = wi_ref[3 * ta + tb]
    span = ch // GROUPS

    def group_of(axis):
        at = lax.broadcasted_iota(jnp.int32, (ch, ch), axis).astype(jnp.float32)
        return jnp.floor((at + 0.5) * (1.0 / span))

    gmat[...] = jnp.where(group_of(0) == group_of(1), 1.0, 0.0).astype(jnp.bfloat16)
    def spot_of(shape, lanes):
        src = lax.broadcasted_iota(jnp.int32, shape, 0)
        dst = lax.broadcasted_iota(jnp.int32, shape, 1) % lanes
        return src, dst, (dst // LAT + 1) % 2 * LAT + dst % LAT

    lane_side = lax.broadcasted_iota(jnp.int32, (8 * LAT, 16 * LAT), 1) // (8 * LAT)
    src, dst, inner = spot_of((8 * LAT, 16 * LAT), 8 * LAT)
    wanted = lane_side * 4 * LAT + dst // (4 * LAT) * 2 * LAT + inner
    pick_own[...] = jnp.where(src == wanted, 1.0, 0.0).astype(jnp.bfloat16)
    block = lax.broadcasted_iota(jnp.int32, (16 * LAT, 24 * LAT), 1) // (8 * LAT)
    src, dst, inner = spot_of((16 * LAT, 24 * LAT), 8 * LAT)
    below = dst // (4 * LAT)
    first_at = jnp.where(below == 0, jnp.where(block == 2, 0, 1 + 2 * block), 0)
    last_at = jnp.where(below == 1, jnp.where(block == 2, 1, 2 * block), 0)
    wanted = below * 8 * LAT + (first_at + last_at) * 2 * LAT + inner
    pick_near[...] = jnp.where(src == wanted, 1.0, 0.0).astype(jnp.bfloat16)
    sums[...] = jnp.zeros_like(sums)
    ubuf[...] = jnp.zeros_like(ubuf)
    dbuf[...] = jnp.zeros_like(dbuf)
    loads[3].wait()
    streamed = dot_t(stream_ref[...], head_ref[...])
    streamed = jnp.concatenate([streamed, jnp.zeros_like(streamed)], axis=1)
    sums[pl.ds(pl.multiple_of(a * tok, 8), tok)] = streamed

    def spread_on(j):
        for d in range(1, BH):
            theirs = lax.rem(bh + BH - d, BH) * 2 + core
            slab = kv.at[j, theirs, 1:A, rows_of_item(j)]
            drain(slab, yrecv.at[j, d])
            remote(slab, slab, csend, crecv.at[j, d], sibling).start()

    for j in range(ITEMS):
        slab = kv.at[j, b, 1:A, rows_of_item(j)]
        drain(slab, zkv.at[j])
        if j + WINDOW < ITEMS + H:
            scatter(j + WINDOW)
        for d in range(1, BH):
            to = a * B + lax.rem(bh + d, BH) * 2 + core
            remote(slab, slab, ysend, yrecv.at[j, d], to).start()
        remote(slab, slab, csend, crecv.at[j, 0], sibling).start()
        if j == LAG - 1:
            for d in range(1, BH):
                theirs = lax.rem(bh + BH - d, BH) * 2 + core
                slab = kv.at[:, theirs, 0]
                drain(slab, yown.at[d])
                remote(slab, slab, csend, cown.at[d], sibling).start()
        if j >= LAG:
            spread_on(j - LAG)
    for j in range(ITEMS + WINDOW, ITEMS + H):
        scatter(j)

    def gathered(j):
        for d in range(BH):
            theirs = lax.rem(bh + BH - d, BH) * 2 + 1 - core
            drain(kv.at[j, theirs, 1:A, rows_of_item(j)], crecv.at[j, d])

    side = lax.broadcasted_iota(jnp.int32, (A * tok, 8 * LAT), 1) // (4 * LAT)

    late = ITEMS - LAG
    for h in range(H):
        while late <= BEFORE[h]:
            spread_on(late)
            late += 1
        if h == 0:
            for d in range(BH):
                theirs = lax.rem(bh + BH - d, BH) * 2 + 1 - core
                drain(kv.at[:, theirs, 0], cown.at[d])
        gathered(key_at(h))
        if h % 2 == 0 and h < H - 1:
            gathered(value_at(h // 2))
        drain(qbuf.at[h], zq.at[h])
        query = qbuf[h].reshape(A * tok, hd)
        if h == H - 1:
            key = jnp.concatenate(
                [
                    kv[key_at(h), :, :, : 2 * cols].reshape(2 * n * cols, hd),
                    kv[key_at(h), :, :, 2 * cols :].reshape(n * cols, hd),
                ],
                axis=0,
            )
        else:
            key = kv[key_at(h)].reshape(n * tok, hd)
        scores = dot_t(query, key)
        top = jnp.max(scores, axis=-1, keepdims=True)
        expo = jnp.exp2((scores - top) * scale)
        total = jnp.sum(expo, axis=-1, keepdims=True)
        weight = expo.astype(jnp.bfloat16)
        if h == H - 1:
            held[...] = weight
            while late < ITEMS:
                spread_on(late)
                late += 1
            gathered(value_at(h // 2))
            value = kv[value_at(h // 2), :, :, : 2 * cols]
            out = jnp.where(
                side == 0,
                dot(held[:, : 2 * n * cols], value.reshape(2 * n * cols, 8 * LAT)),
                dot(held[:, 2 * n * cols :], value[:, :, :cols].reshape(n * cols, 8 * LAT)),
            )
            sums[...] += out / total
        else:
            value = kv[value_at(h // 2)].reshape(n * tok, 8 * LAT)
            out = dot(weight, value) / total
            sums[...] += jnp.where(side == h % 2, out, 0.0)

    whole = sums[...]
    whole = whole + pltpu.roll(whole, 4 * LAT, 1)
    turned = pltpu.roll(whole, 2 * LAT, 1)
    whole = whole.reshape(A, tok, 8 * LAT)
    turned = turned.reshape(A, tok, 8 * LAT)
    left = lax.broadcasted_iota(jnp.int32, (A, 2 * cols, 8 * LAT), 2) < 4 * LAT
    part[...] = jnp.where(left, whole[:, : 2 * cols], whole[:, cols:]).astype(jnp.bfloat16)
    for d in far_first:
        to = lax.rem(a + d, A)
        remote(part.at[to], lbuf.at[a], lsend, lrecv, to * B + b).start()
    quarter_of = lax.broadcasted_iota(jnp.int32, (A, cols, 8 * LAT), 2) // (2 * LAT)
    thirds = [whole[:, i * cols : (i + 1) * cols] for i in range(2)] + [turned[:, 2 * cols :]]
    upper = jnp.where(quarter_of == 1, thirds[0], jnp.where(quarter_of == 3, thirds[1], thirds[2]))
    lower = jnp.where(quarter_of == 0, thirds[0], jnp.where(quarter_of == 2, thirds[1], thirds[2]))
    upart[...] = upper.astype(jnp.bfloat16)
    dpart[...] = lower.astype(jnp.bfloat16)

    def near_rows(act_on):
        for d in far_first + [0]:
            z = lax.rem(a + d, A)
            row = z * B + b

            @pl.when(row < n - 1)
            def _():
                act_on(remote(upart.at[z], ubuf.at[a], usend, urecv, row + 1))

            @pl.when(row > 0)
            def _():
                act_on(remote(dpart.at[z], dbuf.at[a], dsend, drecv, row - 1))

    near_rows(lambda copy: copy.start())
    lbuf[a] = part[a]
    drain(lbuf.at[0 : A - 1], lrecv)

    @pl.when(me > 0)
    def _():
        drain(ubuf, urecv)

    @pl.when(me < n - 1)
    def _():
        drain(dbuf, drecv)

    def total_of(ref):
        total = ref[0].astype(jnp.float32)
        for d in range(1, A):
            total = total + ref[d].astype(jnp.float32)
        return total.astype(jnp.bfloat16)

    laid = dot(total_of(lbuf), pick_own[...])
    own_rows = jnp.concatenate([laid[:, : 8 * LAT], laid[cols:, 8 * LAT :]], axis=0)
    laid = dot(jnp.concatenate([total_of(ubuf), total_of(dbuf)], axis=1), pick_near[...])
    near_lines = jnp.concatenate(
        [laid[:, i * 8 * LAT : (i + 1) * 8 * LAT] for i in range(3)], axis=0
    )
    laid = jnp.concatenate([own_rows, near_lines], axis=0)
    wide = 8 * LAT
    spot = lax.broadcasted_iota(jnp.int32, (2 * tok, wide), 0) % cols
    piece = lax.broadcasted_iota(jnp.int32, (2 * tok, wide), 1) // LAT % 4
    before = jnp.where(spot == 0, 0.0, pltpu.roll(laid, 1, 0))
    after = jnp.where(spot == cols - 1, 0.0, pltpu.roll(laid, 2 * tok - 1, 0))
    laid = jnp.where(piece == 0, before, jnp.where(piece == 3, after, laid)).astype(jnp.bfloat16)
    near = jnp.concatenate([laid[:tok], laid[tok:]], axis=1)
    first[...] = dot(near, w4[2])
    for ta in (1, 0):
        first[(2 - ta) * cols :] += dot(near[: (ta + 1) * cols], w4[ta])

    edge[...] = first[...].astype(jnp.bfloat16)

    def conv(row, phase):
        if row in (1, 2):
            at = ((row - 1) * 2 + phase) * ch
            return first[:, at : at + ch]
        return hbuf[row // 3, :, phase * ch : (phase + 1) * ch].astype(jnp.float32)

    cells = 4 * tok

    def folded(parts):
        whole = parts[0] + parts[1] + parts[2] + parts[3]
        return jnp.sum(whole, axis=0, keepdims=True)

    own = [conv(1 + ri, pc) for ri in range(2) for pc in range(2)]
    mean = folded(own) / cells
    square = folded([(x - mean) * (x - mean) for x in own])
    pieces = ch // 128
    rows = [x[:, 128 * i : 128 * (i + 1)] for x in (mean, square) for i in range(pieces)]
    sbuf[me, : 2 * pieces] = jnp.concatenate(rows, axis=0)

    @pl.loop(1, n)
    def _(d):
        mine = sbuf.at[me, 0 : 2 * pieces]
        remote(mine, mine, ssend, srecv, lax.rem(me + d, n)).start()

    @pl.when(me > 0)
    def _():
        remote(edge.at[:, : 2 * ch], hbuf.at[1], hsend.at[0], hrecv.at[1], me - 1).start()

    @pl.when(me < n - 1)
    def _():
        remote(edge.at[:, 2 * ch :], hbuf.at[0], hsend.at[1], hrecv.at[0], me + 1).start()

    drain(sbuf.at[0 : n - 1, 0 : 2 * pieces], srecv)

    def grouped(x):
        high = x.astype(jnp.bfloat16).astype(jnp.float32)
        rest = x - high
        middle = rest.astype(jnp.bfloat16).astype(jnp.float32)
        pieces = [high, middle, rest - middle, jnp.zeros((13, ch), jnp.float32)]
        split = jnp.concatenate(pieces, axis=0).astype(jnp.bfloat16)
        return jnp.sum(dot(split, gmat[...]), axis=0, keepdims=True)

    means = jnp.concatenate([sbuf[:, i] for i in range(pieces)], axis=1)
    squares = jnp.concatenate([sbuf[:, pieces + i] for i in range(pieces)], axis=1)
    middle = grouped(jnp.sum(means, axis=0, keepdims=True)) / (n * span)
    apart = means - middle
    spread = jnp.sum(squares + cells * (apart * apart), axis=0, keepdims=True)
    variance = grouped(spread) / (n * span * cells)
    root = jnp.sqrt(variance + 1e-06)

    spot = lax.broadcasted_iota(jnp.int32, (tok, ch), 0) % cols

    def place(row, x0, x1):
        left = jnp.where(spot == 0, 0.0, pltpu.roll(x1, 1, 0))
        right = jnp.where(spot == cols - 1, 0.0, pltpu.roll(x0, tok - 1, 0))
        act[:, row, :, 0:ch] = left.astype(jnp.bfloat16).reshape(frames, cols, ch)
        act[:, row, :, 3 * ch :] = right.astype(jnp.bfloat16).reshape(frames, cols, ch)

    loads[4].wait()
    loads[5].wait()
    gain = gain_ref[...].reshape(1, ch)
    shift = shift_ref[...].reshape(1, ch)

    gain = gain / root

    def active(row, phase):
        y = (conv(row, phase) - middle) * gain + shift
        y = y * jax.nn.sigmoid(y)
        if row == 0:
            y = jnp.where(me > 0, y, 0.0)
        if row == 3:
            y = jnp.where(me < n - 1, y, 0.0)
        return y

    def prepare(row):
        x0 = active(row, 0)
        x1 = active(row, 1)
        act[:, row, :, ch : 2 * ch] = x0.astype(jnp.bfloat16).reshape(frames, cols, ch)
        act[:, row, :, 2 * ch : 3 * ch] = x1.astype(jnp.bfloat16).reshape(frames, cols, ch)
        place(row, x0, x1)

    prepare(1)
    prepare(2)
    weights.wait()

    @pl.when(me > 0)
    def _():
        drain(hbuf.at[0], hrecv.at[0])

    @pl.when(me < n - 1)
    def _():
        drain(hbuf.at[1], hrecv.at[1])

    prepare(0)
    prepare(3)

    for ta in (2, 1, 0):
        lines = []
        for f in range(ta + 1):
            for pc in range(2):
                lines.append(
                    jnp.concatenate(
                        [
                            act[f, tb : tb + 2, :, pc * ch : (pc + 3) * ch].reshape(
                                2 * cols, 3 * ch
                            )
                            for tb in range(3)
                        ],
                        axis=1,
                    )
                )
        taken = dot(
            jnp.concatenate(lines, axis=0), wm[3 * ta : 3 * ta + 3].reshape(9 * ch, ch)
        )
        if ta == 2:
            acc[...] = taken
        else:
            acc[(2 - ta) * 4 * cols :] += taken

    for f in range(frames):
        for pc in range(2):
            for ri in range(2):
                at = ((f * 2 + pc) * 2 + ri) * cols
                base = own[2 * ri + pc][f * cols : (f + 1) * cols]
                total = base + acc[at : at + cols]
                lines = pl.ds((f * 2 + ri) * 2 * cols + pc, cols, stride=2)
                for i in range(pieces):
                    woven[i, lines] = total[:, 128 * i : 128 * (i + 1)]
    for i in range(pieces):
        out_ref[:, :, :, 128 * i : 128 * (i + 1)] = (
            woven[i].reshape(frames, 2, 2 * cols, 128).astype(jnp.bfloat16)
        )

    drain(kv.at[0 : ITEMS - 1, 0, 0 : A - 1], zsend.at[0])
    drain(kv.at[ITEMS - 1, 0, 0 : A - 1, rows_of_item(ITEMS - 1)], zsend.at[0])
    drain(qbuf.at[:, 0 : A - 1], zsend.at[1])
    if BH > 1:
        drain(kv.at[0 : ITEMS - 1, 0 : BH - 1], ysend)
        drain(kv.at[ITEMS - 1, 0 : BH - 1, 0], ysend)
        drain(kv.at[ITEMS - 1, 0 : BH - 1, 1:A, rows_of_item(ITEMS - 1)], ysend)
    drain(kv.at[0 : ITEMS - 1, 0:BH], csend)
    drain(kv.at[ITEMS - 1, 0:BH, 0], csend)
    drain(kv.at[ITEMS - 1, 0:BH, 1:A, rows_of_item(ITEMS - 1)], csend)
    drain(part.at[0 : A - 1], lsend)
    drain(sbuf.at[0 : n - 1, 0 : 2 * pieces], ssend)

    near_rows(lambda copy: copy.wait_send())

    @pl.when(me > 0)
    def _():
        drain(hbuf.at[0], hsend.at[0])

    @pl.when(me < n - 1)
    def _():
        drain(hbuf.at[1], hsend.at[1])


def shards(
    n,
    queries,
    keys,
    values,
    stream,
    head_weight,
    conv_in_weight,
    norm_gain,
    norm_shift,
    conv_mid_weight,
):
    frames, rows_here, cols, width = queries.shape
    assert frames == 3 and rows_here == 1
    tok = frames * cols
    hd = width // HEADS
    ch = norm_gain.shape[0]
    A = QUARTERS
    B = n // A
    BH = B // 2
    H = HEADS // A
    PAIRS = (H + 1) // 2
    ITEMS = H + PAIRS
    bf16, f32 = jnp.bfloat16, jnp.float32
    vmem = pl.BlockSpec(memory_space=pltpu.VMEM)
    hbm = pl.BlockSpec(memory_space=pl.ANY)
    dma = pltpu.SemaphoreType.DMA
    operands = [
        pltpu.with_memory_space_constraint(x, pltpu.HBM)
        for x in (
            queries.reshape(tok, width),
            keys.reshape(tok, width),
            values.reshape(tok, width),
            stream.reshape(tok, width),
            head_weight.T,
            conv_in_weight.reshape(9, 3 * LAT, ch),
            norm_gain,
            norm_shift,
            conv_mid_weight.reshape(9, 3 * ch, ch),
        )
    ]
    out = pl.pallas_call(
        functools.partial(body, n, frames, cols),
        out_shape=jax.ShapeDtypeStruct((frames, 2, 2 * cols, ch), bf16),
        in_specs=[hbm] * 9,
        out_specs=vmem,
        scratch_shapes=[
            pltpu.VMEM((tok, width), bf16),
            pltpu.VMEM((ch,), f32),
            pltpu.VMEM((ch,), f32),
            pltpu.VMEM((tok, width), bf16),
            pltpu.VMEM((4 * LAT, width), bf16),
            pltpu.VMEM((9, 3 * LAT, ch), bf16),
            pltpu.VMEM((A, PAIRS, tok, 8 * LAT), bf16),
            pltpu.VMEM((H, A, tok, hd), bf16),
            pltpu.VMEM((ITEMS, B, A, tok, hd), bf16),
            pltpu.VMEM((A * tok, 8 * LAT), f32),
            pltpu.VMEM((A, 2 * cols, 8 * LAT), bf16),
            pltpu.VMEM((A, 2 * cols, 8 * LAT), bf16),
            pltpu.VMEM((A, cols, 8 * LAT), bf16),
            pltpu.VMEM((A, cols, 8 * LAT), bf16),
            pltpu.VMEM((A, cols, 8 * LAT), bf16),
            pltpu.VMEM((A, cols, 8 * LAT), bf16),
            pltpu.VMEM((8 * LAT, 16 * LAT), bf16),
            pltpu.VMEM((16 * LAT, 24 * LAT), bf16),
            pltpu.VMEM((tok, 4 * ch), bf16),
            pltpu.VMEM((2, tok, 2 * ch), bf16),
            pltpu.VMEM((A * tok, n * tok), bf16),
            pltpu.VMEM((3, 16 * LAT, 4 * ch), bf16),
            pltpu.VMEM((9, 3 * ch, ch), bf16),
            pltpu.VMEM((ch, ch), bf16),
            pltpu.VMEM((tok, 4 * ch), f32),
            pltpu.VMEM((frames, 4, cols, 4 * ch), bf16),
            pltpu.VMEM((4 * tok, ch), f32),
            pltpu.VMEM((ch // 128, 4 * tok, 128), f32),
            pltpu.VMEM((n, 8, 128), f32),
            dma((2,)),
            dma((H,)),
            dma((ITEMS,)),
            dma,
            dma,
            dma((ITEMS, BH)),
            dma((BH,)),
            dma((BH,)),
            dma,
            dma,
            dma((ITEMS, BH)),
            dma,
            dma,
            dma,
            dma,
            dma,
            dma,
            dma((2,)),
            dma((2,)),
            dma,
            dma,
            dma,
            dma((6,)),
        ],
        compiler_params=pltpu.CompilerParams(
            collective_id=0, has_side_effects=True, vmem_limit_bytes=44 * 2**20
        ),
        name="decode",
    )(*operands)
    return out


def solution(mesh):
    row = P("groups", "seq", None, None)
    return jax.shard_map(
        functools.partial(shards, mesh.shape["seq"]),
        mesh=mesh,
        in_specs=(row, row, row, row, P(), P(), P(), P(), P()),
        out_specs=row,
        check_vma=False,
    )
```
